512 devices in a mesh: slab: 128 (over y, z, core), sub: 4 (over x).
Axes of the slice: x: 4, y: 4, z: 16, core: 2. Of those that a mesh axis runs over, the one named last changes fastest.
Arguments:
- orbitals: float32 [256, 96, 9216], P('slab', None, 'sub'), may hold values from -6 to 6
- external_potential: float32 [1024, 12288], P('slab', 'sub'), may hold values from -6 to 6
- corners: int32 [256, 2], replicated, may hold values from 0 to 1023, as said below
- pair_list: int32 [256, 2], P('slab'), may hold values from 0 to 255, as said below
- pair_count: int32 [128], P('slab'), may hold values from 1 to 2, as said below
Outputs:
- applied_orbitals: float32 [256, 96, 9216], P('slab', None, 'sub')
The draws below stay inside these ranges and needn't reach their ends.
Inputs may be any that keep to these rules, and one draw needn't show every extreme that they name: `corners`: column 0 is the box's first x plane: for orbital o it lies in the 32 planes that begin at plane 8 * (o // 2), taken mod 1024. Column 1 is the box's first z column (0 to 32). `pair_list`: orbital o is held by slab device o // 2. Rows 2 * d to 2 * d + 1 are the slots of slab device d; in each row (i, j), i is one of device d's orbitals, and j differs from i and is one of device d's orbitals or of device (d + 1) mod 128's. Rows that are not live hold such pairs too. `pair_count`: some slab device has 2 live slots in every draw.
All inputs are finite; a program needn't handle non-finite values.
Results may differ from the reference program's by a relative error of at most 0.0003.
Values sent between devices are 32-bit elements; how exact they have to be, the bound alone decides.
A program may use at most 64 MiB of HBM per device.

```python
import math
import jax
import jax.numpy as jnp
from jax import lax

B = 96
GZ = 128
SX = 8
ORB_DEV = 2
PAIR_MAX = 2
NORB = 256
GX = 1024
SLOTS = 256
N_SLAB = 128


def draw_corners(key, part):
    key_first, key_third = jax.random.split(jax.random.fold_in(key, 11))
    owner_slab = jnp.arange(NORB, dtype=jnp.int32) // ORB_DEV
    jitter = jax.random.randint(key_first, (NORB,), 0, 4 * SX, dtype=jnp.int32)
    first_plane = (owner_slab * SX + jitter) % GX
    third_plane = jax.random.randint(key_third, (NORB,), 0, GZ - B + 1, dtype=jnp.int32)
    return jnp.stack([first_plane, third_plane], axis=1)


def draw_pair_list(key, part):
    key_first, key_stride = jax.random.split(jax.random.fold_in(key, 37))
    owner_slab = jnp.arange(SLOTS, dtype=jnp.int32) // PAIR_MAX
    first_local = jax.random.randint(key_first, (SLOTS,), 0, ORB_DEV, dtype=jnp.int32)
    stride = jax.random.randint(key_stride, (SLOTS,), 1, 2 * ORB_DEV, dtype=jnp.int32)
    second_local = (first_local + stride) % (2 * ORB_DEV)
    first_orbital = owner_slab * ORB_DEV + first_local
    second_orbital = (owner_slab * ORB_DEV + second_local) % NORB
    return jnp.stack([first_orbital, second_orbital], axis=1)


def draw_pair_count(key, part):
    key_busy, key_light, key_top = jax.random.split(jax.random.fold_in(key, 23), 3)
    busy_slab = jax.random.randint(key_busy, (N_SLAB,), 0, 3, dtype=jnp.int32) == 0
    lighter = jax.random.randint(key_light, (N_SLAB,), 1, PAIR_MAX, dtype=jnp.int32)
    counts = jnp.where(busy_slab, PAIR_MAX, lighter).astype(jnp.int32)
    busiest = jax.random.randint(key_top, (), 0, N_SLAB, dtype=jnp.int32)
    return counts.at[busiest].set(PAIR_MAX)


def level_of(stream_key, extent, shards, low, high):
    loudness = 1.0
    for axis_at, shards_of in shards:
        steps = jax.random.uniform(jax.random.fold_in(jax.random.fold_in(stream_key, 6), axis_at), (shards_of,), jnp.float32, low / len(shards), high / len(shards))
        loudness = loudness * jnp.repeat(jnp.exp(steps), extent[axis_at] // shards_of).reshape((-1,) + (1,) * (len(extent) - 1 - axis_at))
    return loudness


def bell_draw(own_key, dims, deviation, bound, pieces=(), kind=jnp.bfloat16):
    drawn = deviation * jax.random.normal(own_key, dims, jnp.float32)
    if pieces:
        drawn = drawn * level_of(own_key, dims, pieces, -0.22, 0.18)
    return jnp.clip(drawn, -bound, bound).astype(kind)


def setup_inputs(seed: int = 0) -> dict:
    key_of = jax.random.split(jax.random.key(seed), 6)
    return {
        "orbitals": bell_draw(key_of[0], (NORB, B, B * B), 1.0, 6.0, ((0, 128), (2, 4)), jnp.float32),
        "external_potential": bell_draw(key_of[1], (GX, B * GZ), 1.0, 6.0, ((0, 128), (1, 4)), jnp.float32),
        "corners": draw_corners(jax.random.fold_in(key_of[5], 71), 0),
        "pair_list": draw_pair_list(jax.random.fold_in(key_of[5], 71), 0),
        "pair_count": draw_pair_count(jax.random.fold_in(key_of[5], 71), 0),
    }


SCREEN = 0.0008
FOCK_SHARE = 0.25
LOCAL_FACTOR = (3.0 / math.pi) ** (1.0 / 3.0)
EPSILON = 1e-06

def sine_table(box_edge):
    levels = jnp.arange(box_edge, dtype=jnp.int32).astype(jnp.float32) + 1.0
    factor = jnp.sqrt(jnp.asarray(2.0 / (box_edge + 1), jnp.float32))
    return factor * jnp.sin(math.pi * levels[:, None] * levels[None, :] / (box_edge + 1))

def sine_levels(box_edge):
    levels = jnp.arange(box_edge, dtype=jnp.int32).astype(jnp.float32) + 1.0
    return 2.0 - 2.0 * jnp.cos(math.pi * levels / (box_edge + 1))

def transform_all(volume, sine_matrix):
    volume = jnp.einsum('ax,xyz->ayz', sine_matrix, volume, precision=lax.Precision.HIGHEST)
    volume = jnp.einsum('by,xyz->xbz', sine_matrix, volume, precision=lax.Precision.HIGHEST)
    return jnp.einsum('cz,xyz->xyc', sine_matrix, volume, precision=lax.Precision.HIGHEST)

def solve_box(density):
    box_edge = density.shape[0]
    sine_matrix = sine_table(box_edge)
    levels = sine_levels(box_edge)
    kernel = 4.0 * math.pi / (levels[:, None, None] + levels[None, :, None] + levels[None, None, :] + SCREEN)
    return transform_all(kernel * transform_all(density, sine_matrix), sine_matrix)

def move_box(volume, shift_first, shift_third):
    box_edge = volume.shape[0]
    depth = volume.shape[2]
    first_source = jnp.arange(box_edge, dtype=jnp.int32) - shift_first.astype(jnp.int32)
    first_keep = ((first_source >= 0) & (first_source < box_edge)).astype(jnp.float32)
    volume = jnp.take(volume, jnp.clip(first_source, 0, box_edge - 1).astype(jnp.int32), axis=0) * first_keep[:, None, None]
    third_source = jnp.arange(depth, dtype=jnp.int32) - shift_third.astype(jnp.int32)
    third_keep = ((third_source >= 0) & (third_source < depth)).astype(jnp.float32)
    return jnp.take(volume, jnp.clip(third_source, 0, depth - 1).astype(jnp.int32), axis=2) * third_keep[None, None, :]

def pair_shifts(corner_first, corner_second, grid_planes):
    half_span = grid_planes // 2
    shift_first = (corner_second[0] - corner_first[0] + half_span) % grid_planes - half_span
    shift_third = corner_second[1] - corner_first[1]
    return (shift_first, shift_third)

def laplace_box(volume):
    padded = jnp.pad(volume, 1)
    beside_all = padded[2:, 1:-1, 1:-1] + padded[:-2, 1:-1, 1:-1]
    beside_all = beside_all + padded[1:-1, 2:, 1:-1] + padded[1:-1, :-2, 1:-1]
    beside_all = beside_all + padded[1:-1, 1:-1, 2:] + padded[1:-1, 1:-1, :-2]
    return beside_all - 6.0 * volume

def reference(orbitals, external_potential, corners, pair_list, pair_count):
    box_edge = orbitals.shape[1]
    boxes = orbitals.reshape(orbitals.shape[0], box_edge, box_edge, box_edge)
    grid_planes = external_potential.shape[0]
    grid_depth = external_potential.shape[1] // box_edge
    zero_index = jnp.zeros((), jnp.int32)
    offsets = jnp.arange(box_edge, dtype=jnp.int32)

    def deposit(density_grid, scan_item):
        volume, corner = scan_item
        placed = lax.dynamic_update_slice(jnp.zeros((box_edge, box_edge, grid_depth), jnp.float32), volume * volume, (zero_index, zero_index, corner[1].astype(jnp.int32)))
        planes = (corner[0] + offsets) % grid_planes
        return (density_grid.at[planes].add(placed.reshape(box_edge, box_edge * grid_depth)), None)
    density, _ = lax.scan(deposit, jnp.zeros((grid_planes, box_edge * grid_depth), jnp.float32), (boxes, corners))
    local_field = external_potential - LOCAL_FACTOR * jnp.cbrt(density + EPSILON)
    live_slots = (jnp.arange(PAIR_MAX, dtype=jnp.int32)[None, :] < pair_count[:, None]).astype(jnp.float32).reshape(-1)

    def one_pair(fock_terms, scan_item):
        pair_row, weight = scan_item
        first_orbital = pair_row[0]
        second_orbital = pair_row[1]
        shift_first, shift_third = pair_shifts(corners[first_orbital], corners[second_orbital], grid_planes)
        box_first = boxes[first_orbital]
        moved_box = move_box(boxes[second_orbital], shift_first, shift_third)
        potential = solve_box(box_first * moved_box)
        fock_terms = fock_terms.at[first_orbital].add(weight * potential * moved_box)
        fock_terms = fock_terms.at[second_orbital].add(weight * move_box(potential * box_first, -shift_first, -shift_third))
        return (fock_terms, None)
    exchange_field, _ = lax.scan(one_pair, jnp.zeros_like(boxes), (pair_list, live_slots))

    def finish(scan_item):
        volume, corner, exchange = scan_item
        planes = (corner[0] + offsets) % grid_planes
        taken = jnp.take(local_field, planes, axis=0).reshape(box_edge, box_edge, grid_depth)
        box_local = lax.dynamic_slice_in_dim(taken, corner[1].astype(jnp.int32), box_edge, 2)
        return -0.5 * laplace_box(volume) + box_local * volume - FOCK_SHARE * exchange
    result = lax.map(finish, (boxes, corners, exchange_field))
    return result.reshape(orbitals.shape)
```

```python
import functools
import math

import jax
import jax.numpy as jnp
import ml_dtypes
import numpy as np
from jax import lax
from jax.experimental import pallas as pl
from jax.experimental.pallas import tpu as pltpu
from jax.sharding import PartitionSpec as P

SCREEN = 0.0008
FOCK_SHARE = 0.25
LOCAL_FACTOR = (3.0 / math.pi) ** (1.0 / 3.0)
EPSILON = 1e-06

B = 96
ROWS = 24
GZ = 128
SX = 8
REACH = 16
SUBS = 4
GROUP = 4
CHUNKS = ROWS // GROUP
LANES = GROUP * B
GLANES = GROUP * GZ
EDGE = 128
RING = 3
RL = ROWS * GZ // RING

F32 = jnp.float32
BF16 = jnp.bfloat16
MESH = pl.DeviceIdType.MESH


def halves(value):
    high = value.astype(ml_dtypes.bfloat16)
    low = (value - high.astype(np.float64)).astype(ml_dtypes.bfloat16)
    return high, low


def tables():
    level = np.arange(B, dtype=np.float64) + 1.0
    sine = math.sqrt(2.0 / (B + 1)) * np.sin(math.pi * level[:, None] * level[None, :] / (B + 1))
    eigen = 2.0 - 2.0 * np.cos(math.pi * level / (B + 1))
    high, low = halves(sine)
    left = np.concatenate([high, low], axis=0)
    wide = np.zeros((LANES, GLANES), np.float64)
    for k in range(GROUP):
        wide[k * B : (k + 1) * B, k * GZ : k * GZ + B] = sine
    wide_high, wide_low = halves(wide)
    narrow_high, narrow_low = wide_high.T.copy(), wide_low.T.copy()
    rows = np.arange(LANES + 2 * EDGE)[:, None] - EDGE
    cols = np.arange(LANES)[None, :]
    beside = np.abs(rows - cols)
    near = (beside == B) | ((beside == 1) & (rows // B == cols // B))
    near = near.astype(ml_dtypes.bfloat16)
    line = np.abs(np.arange(B)[:, None] - np.arange(B)[None, :])
    column = ((line == 1) * 1.0 - (line == 0) * 6.0).astype(ml_dtypes.bfloat16)
    level_bc = np.ones((B, GZ), np.float64)
    level_bc[:, :B] = eigen[:, None] + eigen[None, :] + SCREEN
    return (
        left,
        wide_high,
        wide_low,
        narrow_high,
        narrow_low,
        near,
        column,
        level_bc.astype(np.float32),
        eigen.astype(np.float32),
    )


def split(value):
    high = value.astype(BF16)
    low = (value - high.astype(F32)).astype(BF16)
    return high, low


def dot(a, b):
    return jnp.dot(a, b, preferred_element_type=F32)


def left3(pair, value):
    high, low = split(value)
    both = dot(pair, high)
    return both[:B] + both[B:] + dot(pair[:B], low)


def right3(value, t_high, t_low):
    high, low = split(value)
    return dot(high, t_high) + dot(low, t_high) + dot(high, t_low)


def right1(value, table):
    high, low = split(value)
    return dot(high, table) + dot(low, table)


def left1(table, value):
    high, low = split(value)
    return dot(table, high) + dot(table, low)


def iotas(rows, cols):
    return (
        lax.broadcasted_iota(jnp.int32, (rows, cols), 0),
        lax.broadcasted_iota(jnp.int32, (rows, cols), 1),
    )


def band(index):
    one = jnp.int32(1)
    zero = jnp.int32(0)
    total = jnp.zeros_like(index)
    for k in range(1, GROUP):
        total = total + jnp.where(index >= k * B, one, zero)
    return total


def hot(condition):
    return jnp.where(condition, 1.0, 0.0).astype(BF16)


def kernel(
    slabs,
    corners,
    pairs,
    count,
    eigen,
    orb,
    ext,
    left,
    wide_h,
    wide_l,
    narrow_h,
    narrow_l,
    near,
    column,
    level_bc,
    out,
    obx,
    nxt,
    moved,
    spec,
    pencil,
    turned,
    solved,
    win,
    rbk,
    fw,
    exch,
    ret,
    back,
    dz_to,
    dz_from,
    dx_to,
    dx_from,
    put_z,
    get_z,
    put_x,
    get_x,
    load_sem,
    box_s,
    box_r,
    halo_s,
    halo_r,
    one_s,
    one_r,
    one_o,
    two_s,
    two_r,
    two_o,
    ret_s,
    ret_r,
    den_s,
    den_r,
    fld_s,
    fld_r,
):
    slab = lax.axis_index("slab")
    sub = lax.axis_index("sub")
    ahead = lax.rem(slab + 1, slabs)
    behind = lax.rem(slab + slabs - 1, slabs)
    planes = slabs * SX
    orbitals = 2 * slabs

    barrier = pltpu.get_barrier_semaphore()
    load = pltpu.make_async_copy(orb, obx.at[:, :, EDGE : EDGE + ROWS * B], load_sem)
    load.start()
    for who in (ahead, behind):
        pl.semaphore_signal(barrier, inc=1, device_id=(who, sub), device_id_type=MESH)
    for k in range(1, SUBS):
        pl.semaphore_signal(
            barrier, inc=1, device_id=(slab, lax.rem(sub + k, SUBS)), device_id_type=MESH
        )
    pl.semaphore_wait(barrier, 2 + SUBS - 1)

    def box_copy(g):
        return pltpu.make_async_remote_copy(
            src_ref=obx.at[:, :, pl.ds(pl.multiple_of(EDGE + g * LANES, 128), LANES)],
            dst_ref=nxt.at[:, :, pl.ds(pl.multiple_of(g * LANES, 128), LANES)],
            send_sem=box_s.at[g],
            recv_sem=box_r.at[g],
            device_id=(behind, sub),
            device_id_type=MESH,
        )

    def halo_copy(side):
        start = EDGE if side == 0 else ROWS * B
        land = EDGE + ROWS * B if side == 0 else 0
        who = lax.rem(sub + (SUBS - 1 if side == 0 else 1), SUBS)
        return pltpu.make_async_remote_copy(
            src_ref=obx.at[:, :, start : start + EDGE],
            dst_ref=obx.at[:, :, land : land + EDGE],
            send_sem=halo_s.at[side],
            recv_sem=halo_r.at[side],
            device_id=(slab, who),
            device_id_type=MESH,
        )

    def rows_of(g):
        return pl.ds(pl.multiple_of(g * GROUP * ROWS, 8), GROUP * ROWS)

    def one_copy(k, g):
        who = lax.rem(sub + k, SUBS)
        return pltpu.make_async_remote_copy(
            src_ref=spec.at[:, who, rows_of(g)],
            dst_ref=pencil.at[:, sub, rows_of(g)],
            send_sem=one_s.at[k - 1, g],
            recv_sem=one_r.at[k - 1, g],
            device_id=(slab, who),
            device_id_type=MESH,
        )

    def two_copy(k, g):
        who = lax.rem(sub + k, SUBS)
        return pltpu.make_async_remote_copy(
            src_ref=turned.at[:, who, rows_of(g)],
            dst_ref=solved.at[:, sub, rows_of(g)],
            send_sem=two_s.at[k - 1, g],
            recv_sem=two_r.at[k - 1, g],
            device_id=(slab, who),
            device_id_type=MESH,
        )

    def one_own(g):
        return pltpu.make_async_copy(
            spec.at[:, sub, rows_of(g)], pencil.at[:, sub, rows_of(g)], one_o.at[g]
        )

    def two_own(g):
        return pltpu.make_async_copy(
            turned.at[:, sub, rows_of(g)], solved.at[:, sub, rows_of(g)], two_o.at[g]
        )

    def ret_copy(g):
        lanes = pl.ds(pl.multiple_of(g * LANES, 128), LANES)
        return pltpu.make_async_remote_copy(
            src_ref=ret.at[:, :, lanes],
            dst_ref=back.at[:, :, lanes],
            send_sem=ret_s.at[g],
            recv_sem=ret_r.at[g],
            device_id=(ahead, sub),
            device_id_type=MESH,
        )

    def den_copy(step, c):
        lanes = pl.ds(c * RL, RL)
        return pltpu.make_async_remote_copy(
            src_ref=win.at[REACH - step, :, lanes],
            dst_ref=rbk.at[step - 1, :, lanes],
            send_sem=den_s.at[step - 1, c],
            recv_sem=den_r.at[step - 1, c],
            device_id=(ahead, sub),
            device_id_type=MESH,
        )

    def fld_copy(step, c):
        lanes = pl.ds(c * RL, RL)
        return pltpu.make_async_remote_copy(
            src_ref=fw.at[step - 1, :, lanes],
            dst_ref=fw.at[step, :, lanes],
            send_sem=fld_s.at[step - 1, c],
            recv_sem=fld_r.at[step - 1, c],
            device_id=(behind, sub),
            device_id_type=MESH,
        )

    start_x = []
    start_z = []
    for o in range(2):
        mine = slab * 2 + o
        start_x.append(lax.rem(corners[2 * mine] - slab * SX + planes, planes))
        start_z.append(corners[2 * mine + 1])
    first, second, weight, shift_x, shift_z = [], [], [], [], []
    for s in range(2):
        i, j = pairs[s, 0], pairs[s, 1]
        first.append(lax.rem(i - 2 * slab + orbitals, orbitals))
        second.append(lax.rem(j - 2 * slab + orbitals, orbitals))
        half = planes // 2
        shift_x.append(
            lax.rem(corners[2 * j] - corners[2 * i] + half + planes, planes) - half
        )
        shift_z.append(corners[2 * j + 1] - corners[2 * i + 1])
        weight.append(jnp.where(count[0] > s, jnp.float32(1.0), jnp.float32(0.0)))

    load.wait()

    def send_boxes(g, _):
        box_copy(g).start()
        return 0

    lax.fori_loop(0, CHUNKS, send_boxes, 0)
    halo_copy(0).start()
    halo_copy(1).start()

    row, col = iotas(LANES, GLANES)
    at = row + 32 * band(row)
    for o in range(2):
        put_z[o] = hot(col - at == start_z[o])
    row, col = iotas(REACH * SX, B)
    for o in range(2):
        put_x[o] = hot(row - col == start_x[o])

    def deposit(g, _):
        lanes = pl.ds(pl.multiple_of(EDGE + g * LANES, 128), LANES)
        total = None
        for o in range(2):
            box = obx[o, :, lanes]
            wide = right1(box * box, put_z[o])
            part = left1(put_x[o], wide)
            total = part if total is None else total + part
        grid = pl.ds(pl.multiple_of(g * GLANES, 128), GLANES)
        win[:, :, grid] = total.reshape(REACH, SX, GLANES)
        return 0

    lax.fori_loop(0, CHUNKS, deposit, 0)
    for c in range(RING):
        den_copy(1, c).start()

    def density_step(step):
        for c in range(RING):
            lanes = pl.ds(c * RL, RL)
            den_copy(step - 1, c).wait_recv()
            win[REACH - step, :, lanes] += rbk[step - 2, :, lanes]
            den_copy(step, c).start()

    row, col = iotas(LANES, LANES)
    same = band(row) == band(col)
    for s in range(2):
        dz_to[s] = hot(same & (col - row == shift_z[s]))
        dz_from[s] = hot(same & (row - col == shift_z[s]))
    row, col = iotas(B, B)
    for s in range(2):
        dx_to[s] = hot(row - col == shift_x[s])
        dx_from[s] = hot(col - row == shift_x[s])
    row, col = iotas(GLANES, LANES)
    at = col + 32 * band(col)
    for o in range(2):
        get_z[o] = hot(row - at == start_z[o])
    row, col = iotas(B, REACH * SX)
    for o in range(2):
        get_x[o] = hot(col - row == start_x[o])

    def forward(g, _):
        density_step(2 + 2 * g)
        density_step(3 + 2 * g)
        box_copy(g).wait_recv()
        lanes = pl.ds(pl.multiple_of(g * LANES, 128), LANES)
        own = pl.ds(pl.multiple_of(EDGE + g * LANES, 128), LANES)
        for s in range(2):
            boxes = [obx[0, :, own], obx[1, :, own]]
            other = jnp.where(
                second[s] < 2,
                jnp.where(second[s] == 0, boxes[0], boxes[1]),
                jnp.where(second[s] == 2, nxt[0, :, lanes], nxt[1, :, lanes]),
            )
            shifted = left1(dx_to[s], right1(other, dz_to[s]))
            moved[s, :, lanes] = shifted
            rho = jnp.where(first[s] == 0, boxes[0], boxes[1]) * shifted
            wide = right3(rho, wide_h[...], wide_l[...])
            for k in range(0, GROUP, 2):
                two = left3(left[...], wide[:, k * GZ : (k + 2) * GZ])
                for m in range(2):
                    for q in range(SUBS):
                        spec[s, q, pl.ds(pl.multiple_of((g * GROUP + k + m) * ROWS, 8), ROWS), :] = (
                            two[q * ROWS : (q + 1) * ROWS, m * GZ : (m + 1) * GZ]
                        )
        for k in (2, 1, 3):
            one_copy(k, g).start()
        one_own(g).start()
        return 0

    lax.fori_loop(0, CHUNKS, forward, 0)
    density_step(14)
    density_step(15)

    for c in range(RING):
        lanes = pl.ds(c * RL, RL)
        den_copy(15, c).wait_recv()
        value = win[0, :, lanes] + rbk[14, :, lanes] + EPSILON
        root = jnp.exp(jnp.log(value) * (1.0 / 3.0))
        root = root - (root * root * root - value) / (3.0 * root * root)
        fw[0, :, lanes] = ext[:, lanes] - LOCAL_FACTOR * root
        fld_copy(1, c).start()

    def field_step(step):
        for c in range(RING):
            fld_copy(step - 1, c).wait_recv()
            fld_copy(step, c).start()

    def wait_one(g, _):
        for k in range(1, SUBS):
            one_copy(k, g).wait_recv()
        one_own(g).wait()
        return 0

    lax.fori_loop(0, CHUNKS, wait_one, 0)

    def along_y(t, _):
        a = 2 * t
        pieces = []
        for m in range(2):
            level = eigen[sub * ROWS + a + m]
            pieces.append((4.0 * math.pi) / (level_bc[...] + level))
        factor = jnp.concatenate(pieces, axis=1)
        for s in range(2):
            parts = []
            for m in range(2):
                parts.append(
                    jnp.concatenate(
                        [pencil[s, q, pl.ds(a + m, ROWS, stride=ROWS), :] for q in range(SUBS)],
                        axis=0,
                    )
                )
            value = jnp.concatenate(parts, axis=1)
            value = left3(left[...], factor * left3(left[...], value))
            for m in range(2):
                for q in range(SUBS):
                    turned[s, q, pl.ds(a + m, ROWS, stride=ROWS), :] = value[
                        q * ROWS : (q + 1) * ROWS, m * GZ : (m + 1) * GZ
                    ]
        field_step(2 + t)
        return 0

    lax.fori_loop(0, ROWS // 2, along_y, 0)

    def send_two(g, _):
        for k in (2, 1, 3):
            two_copy(k, g).start()
        two_own(g).start()
        return 0

    lax.fori_loop(0, CHUNKS, send_two, 0)
    field_step(14)
    field_step(15)
    halo_copy(0).wait_recv()
    halo_copy(1).wait_recv()
    keep_low = jnp.where(sub > 0, jnp.float32(1.0), jnp.float32(0.0))
    keep_high = jnp.where(sub < SUBS - 1, jnp.float32(1.0), jnp.float32(0.0))
    obx[:, :, 0:EDGE] = obx[:, :, 0:EDGE] * keep_low
    high_edge = EDGE + ROWS * B
    obx[:, :, high_edge : high_edge + EDGE] = obx[:, :, high_edge : high_edge + EDGE] * keep_high

    def inverse(g, _):
        for k in range(1, SUBS):
            two_copy(k, g).wait_recv()
        two_own(g).wait()
        lanes = pl.ds(pl.multiple_of(g * LANES, 128), LANES)
        own = pl.ds(pl.multiple_of(EDGE + g * LANES, 128), LANES)
        boxes = [obx[0, :, own], obx[1, :, own]]
        mine = [None, None]
        theirs = [None, None]

        def add(held, k, value):
            held[k] = value if held[k] is None else held[k] + value

        for s in range(2):
            parts = []
            for k in range(0, GROUP, 2):
                pieces = []
                for m in range(2):
                    rows = pl.ds(pl.multiple_of((g * GROUP + k + m) * ROWS, 8), ROWS)
                    pieces.append(
                        jnp.concatenate([solved[s, q, rows, :] for q in range(SUBS)], axis=0)
                    )
                parts.append(left3(left[...], jnp.concatenate(pieces, axis=1)))
            potential = right3(jnp.concatenate(parts, axis=1), narrow_h[...], narrow_l[...])
            potential = potential * weight[s]
            onto_first = potential * moved[s, :, lanes]
            onto_second = left1(
                dx_from[s], right1(
                    potential * jnp.where(first[s] == 0, boxes[0], boxes[1]), dz_from[s]
                ),

            )
            for k in range(2):
                add(mine, k, jnp.where(first[s] == k, onto_first, 0.0))
                add(mine, k, jnp.where(second[s] == k, onto_second, 0.0))
                add(theirs, k, jnp.where(second[s] == 2 + k, onto_second, 0.0))
        for k in range(2):
            exch[k, :, lanes] = mine[k]
            ret[k, :, lanes] = theirs[k]
        ret_copy(g).start()
        return 0

    lax.fori_loop(0, CHUNKS, inverse, 0)
    for c in range(RING):
        fld_copy(15, c).wait_recv()

    def finish(g, _):
        lanes = pl.ds(pl.multiple_of(g * LANES, 128), LANES)
        own = pl.ds(pl.multiple_of(EDGE + g * LANES, 128), LANES)
        around = pl.ds(pl.multiple_of(g * LANES, 128), LANES + 2 * EDGE)
        grid = pl.ds(pl.multiple_of(g * GLANES, 128), GLANES)
        field = fw[:, :, grid].reshape(REACH * SX, GLANES)
        ret_copy(g).wait_recv()
        for o in range(2):
            box = obx[o, :, own]
            local = right1(left1(get_x[o], field), get_z[o])
            lap = right1(obx[o, :, around], near[...]) + left1(column[...], box)
            out[o, :, lanes] = (
                -0.5 * lap + local * box - FOCK_SHARE * (exch[o, :, lanes] + back[o, :, lanes])
            )
        return 0

    lax.fori_loop(0, CHUNKS, finish, 0)

    def drain(g, _):
        box_copy(g).wait_send()
        ret_copy(g).wait_send()
        for k in range(1, SUBS):
            one_copy(k, g).wait_send()
            two_copy(k, g).wait_send()
        return 0

    lax.fori_loop(0, CHUNKS, drain, 0)
    halo_copy(0).wait_send()
    halo_copy(1).wait_send()

    def drain_ring(step, _):
        for c in range(RING):
            den_copy(step, c).wait_send()
            fld_copy(step, c).wait_send()
        return 0

    lax.fori_loop(1, REACH, drain_ring, 0)


def local(slabs, orbitals, external_potential, corners, pair_list, pair_count):
    vmem = pl.BlockSpec(memory_space=pltpu.VMEM)
    smem = pl.BlockSpec(memory_space=pltpu.SMEM)
    table = tables()
    arrays = [jnp.asarray(t) for t in table[:-1]]
    eigen = jnp.asarray(table[-1])
    dma = pltpu.SemaphoreType.DMA
    part = (2, B, ROWS * B)
    turns = (2, SUBS, ROWS * ROWS, GZ)
    return pl.pallas_call(
        functools.partial(kernel, slabs),
        out_shape=jax.ShapeDtypeStruct(orbitals.shape, F32),
        in_specs=[smem] * 4 + [pl.BlockSpec(memory_space=pl.ANY)] + [vmem] * (1 + len(arrays)),
        out_specs=vmem,
        scratch_shapes=[
            pltpu.VMEM((2, B, ROWS * B + 2 * EDGE), F32),
            pltpu.VMEM(part, F32),
            pltpu.VMEM(part, F32),
            pltpu.VMEM(turns, F32),
            pltpu.VMEM(turns, F32),
            pltpu.VMEM(turns, F32),
            pltpu.VMEM(turns, F32),
            pltpu.VMEM((REACH, SX, ROWS * GZ), F32),
            pltpu.VMEM((REACH - 1, SX, ROWS * GZ), F32),
            pltpu.VMEM((REACH, SX, ROWS * GZ), F32),
            pltpu.VMEM(part, F32),
            pltpu.VMEM(part, F32),
            pltpu.VMEM(part, F32),
            pltpu.VMEM((2, LANES, LANES), BF16),
            pltpu.VMEM((2, LANES, LANES), BF16),
            pltpu.VMEM((2, B, B), BF16),
            pltpu.VMEM((2, B, B), BF16),
            pltpu.VMEM((2, LANES, GLANES), BF16),
            pltpu.VMEM((2, GLANES, LANES), BF16),
            pltpu.VMEM((2, REACH * SX, B), BF16),
            pltpu.VMEM((2, B, REACH * SX), BF16),
            dma,
            dma((CHUNKS,)),
            dma((CHUNKS,)),
            dma((2,)),
            dma((2,)),
            dma((SUBS - 1, CHUNKS)),
            dma((SUBS - 1, CHUNKS)),
            dma((CHUNKS,)),
            dma((SUBS - 1, CHUNKS)),
            dma((SUBS - 1, CHUNKS)),
            dma((CHUNKS,)),
            dma((CHUNKS,)),
            dma((CHUNKS,)),
            dma((REACH - 1, RING)),
            dma((REACH - 1, RING)),
            dma((REACH - 1, RING)),
            dma((REACH - 1, RING)),
        ],
        compiler_params=pltpu.CompilerParams(
            collective_id=0, has_side_effects=True, vmem_limit_bytes=60 * 1024 * 1024
        ),
        name="orbitals",
    )(corners.reshape(-1), pair_list, pair_count, eigen, orbitals, external_potential, *arrays)


def solution(mesh):
    placed = (P("slab", None, "sub"), P("slab", "sub"), P(), P("slab", None), P("slab"))
    return jax.shard_map(
        functools.partial(local, mesh.shape["slab"]),
        mesh=mesh,
        in_specs=placed,
        out_specs=P("slab", None, "sub"),
        check_vma=False,
    )
```

```python
import functools
import math

import jax
import jax.numpy as jnp
import ml_dtypes
import numpy as np
from jax import lax
from jax.experimental import pallas as pl
from jax.experimental.pallas import tpu as pltpu
from jax.sharding import PartitionSpec as P

SCREEN = 0.0008
FOCK_SHARE = 0.25
LOCAL_FACTOR = (3.0 / math.pi) ** (1.0 / 3.0)
EPSILON = 1e-06

B = 96
ROWS = 24
GZ = 128
SX = 8
REACH = 16
SUBS = 4
GROUP = 4
CHUNKS = ROWS // GROUP
LANES = GROUP * B
GLANES = GROUP * GZ
EDGE = 128
RING = 3
RL = ROWS * GZ // RING
HOPS = REACH // 2
OCTS = ROWS // 8

F32 = jnp.float32
BF16 = jnp.bfloat16
MESH = pl.DeviceIdType.MESH


def halves(value):
    high = value.astype(ml_dtypes.bfloat16)
    low = (value - high.astype(np.float64)).astype(ml_dtypes.bfloat16)
    return high, low


def tables():
    level = np.arange(B, dtype=np.float64) + 1.0
    sine = math.sqrt(2.0 / (B + 1)) * np.sin(math.pi * level[:, None] * level[None, :] / (B + 1))
    eigen = 2.0 - 2.0 * np.cos(math.pi * level / (B + 1))
    high, low = halves(sine)
    left = np.block([[high, high], [low, np.zeros_like(low)]])
    wide = np.zeros((LANES, GLANES), np.float64)
    for k in range(GROUP):
        wide[k * B : (k + 1) * B, k * GZ : k * GZ + B] = sine
    wide_high, wide_low = halves(wide)
    narrow_high, narrow_low = wide_high.T.copy(), wide_low.T.copy()
    rows = np.arange(LANES + 2 * EDGE)[:, None] - EDGE
    cols = np.arange(LANES)[None, :]
    beside = np.abs(rows - cols)
    near = (beside == B) | ((beside == 1) & (rows // B == cols // B))
    near = near.astype(ml_dtypes.bfloat16)
    line = np.abs(np.arange(B)[:, None] - np.arange(B)[None, :])
    column = ((line == 1) * 1.0 - (line == 0) * 6.0).astype(ml_dtypes.bfloat16)
    column = np.concatenate([column, column], axis=1)
    level_bc = np.ones((B, GZ), np.float64)
    level_bc[:, :B] = eigen[:, None] + eigen[None, :] + SCREEN
    return (
        left,
        wide_high,
        wide_low,
        narrow_high,
        narrow_low,
        near,
        column,
        level_bc.astype(np.float32),
        eigen.astype(np.float32),
    )


def split(value):
    high = value.astype(BF16)
    low = (value - high.astype(F32)).astype(BF16)
    return high, low


def stack(value):
    return jnp.concatenate(split(value), axis=0)


def dot(a, b):
    return jnp.dot(a, b, preferred_element_type=F32)


def left3(table, value):
    both = dot(table, stack(value))
    return both[:B] + both[B:]


def right3(values, t_high, t_low):
    parts = [split(v) for v in values]
    rows = values[0].shape[0]
    count = len(values)
    high = jnp.concatenate([p[0] for p in parts], axis=0)
    full = dot(jnp.concatenate([high] + [p[1] for p in parts], axis=0), t_high)
    rest = dot(high, t_low)
    return [
        full[k * rows : (k + 1) * rows]
        + full[(count + k) * rows : (count + k + 1) * rows]
        + rest[k * rows : (k + 1) * rows]
        for k in range(count)
    ]


def right1(value, table):
    rows = value.shape[0]
    both = dot(stack(value), table)
    return both[:rows] + both[rows:]


def pick1(value, table):
    return dot(stack(value), table).astype(BF16)


def iotas(rows, cols):
    return (
        lax.broadcasted_iota(jnp.int32, (rows, cols), 0),
        lax.broadcasted_iota(jnp.int32, (rows, cols), 1),
    )


def band(index):
    one = jnp.int32(1)
    zero = jnp.int32(0)
    total = jnp.zeros_like(index)
    for k in range(1, GROUP):
        total = total + jnp.where(index >= k * B, one, zero)
    return total


def hot(condition):
    return jnp.where(condition, 1.0, 0.0).astype(BF16)


def twice(table):
    return jnp.concatenate([table, table], axis=1)


def kernel(
    slabs,
    corners,
    pairs,
    count,
    eigen,
    orb,
    ext,
    left,
    wide_h,
    wide_l,
    narrow_h,
    narrow_l,
    near,
    column,
    level_bc,
    out,
    obx,
    nxt,
    moved,
    spec,
    pencil,
    turned,
    solved,
    win,
    mate,
    came,
    fw,
    ret,
    back,
    dz_to,
    dz_from,
    dx_to,
    dx_from,
    put_z,
    get_z,
    put_x,
    get_x,
    load_sem,
    box_s,
    box_r,
    halo_s,
    halo_r,
    one_s,
    one_r,
    one_o,
    two_s,
    two_r,
    two_o,
    ret_s,
    ret_r,
    mate_s,
    mate_r,
    den_s,
    den_r,
    fld_s,
    fld_r,
    give_s,
    give_r,
):
    slab = lax.axis_index("slab")
    sub = lax.axis_index("sub")
    ahead = lax.rem(slab + 1, slabs)
    behind = lax.rem(slab + slabs - 1, slabs)
    ahead2 = lax.rem(slab + 2, slabs)
    behind2 = lax.rem(slab + slabs - 2, slabs)
    odd = lax.rem(slab, 2)
    partner = slab + 1 - 2 * odd
    planes = slabs * SX
    orbitals = 2 * slabs

    load = pltpu.make_async_copy(orb, obx.at[:, :, EDGE : EDGE + ROWS * B], load_sem)
    load.start()
    mate[0] = jnp.zeros((SX, ROWS * GZ), F32)
    mate[HOPS] = jnp.zeros((SX, ROWS * GZ), F32)
    win[REACH] = jnp.zeros((SX, ROWS * GZ), F32)
    barrier = pltpu.get_barrier_semaphore()
    for who in (ahead, behind, ahead2, behind2):
        pl.semaphore_signal(barrier, inc=1, device_id=(who, sub), device_id_type=MESH)
    for k in range(1, SUBS):
        pl.semaphore_signal(
            barrier, inc=1, device_id=(slab, lax.rem(sub + k, SUBS)), device_id_type=MESH
        )

    def remote(src, dst, send, recv, who):
        return pltpu.make_async_remote_copy(
            src_ref=src,
            dst_ref=dst,
            send_sem=send,
            recv_sem=recv,
            device_id=who,
            device_id_type=MESH,
        )

    def box_lanes(g):
        return pl.ds(pl.multiple_of(g * LANES, 128), LANES)

    def own_lanes(g):
        return pl.ds(pl.multiple_of(EDGE + g * LANES, 128), LANES)

    def grid_lanes(g):
        return pl.ds(pl.multiple_of(g * GLANES, 128), GLANES)

    def box_copy(g):
        return remote(
            obx.at[:, :, own_lanes(g)],
            nxt.at[:, :, box_lanes(g)],
            box_s,
            box_r.at[g],
            (behind, sub),
        )

    def halo_copy(side):
        start = EDGE if side == 0 else ROWS * B
        land = EDGE + ROWS * B if side == 0 else 0
        who = lax.rem(sub + (SUBS - 1 if side == 0 else 1), SUBS)
        return remote(
            obx.at[:, :, start : start + EDGE],
            obx.at[:, :, land : land + EDGE],
            halo_s.at[side],
            halo_r.at[side],
            (slab, who),
        )

    def rows_of(g):
        return pl.ds(pl.multiple_of(g * GROUP * ROWS, 8), GROUP * ROWS)

    def one_copy(k, g):
        who = lax.rem(sub + k, SUBS)
        return remote(
            spec.at[:, who, rows_of(g)],
            pencil.at[:, sub, rows_of(g)],
            one_s.at[k - 1],
            one_r.at[k - 1, g],
            (slab, who),
        )

    def one_own(g):
        return pltpu.make_async_copy(
            spec.at[:, sub, rows_of(g)], pencil.at[:, sub, rows_of(g)], one_o.at[g]
        )

    def piece(e, g):
        if g is None:
            return pl.ds(0, ROWS * 8)
        return pl.ds(pl.multiple_of(g * GROUP * 8, 8), GROUP * 8)

    def slot(e, g):
        return e if g is None else OCTS - 1 + g

    def two_copy(k, e, g):
        who = lax.rem(sub + k, SUBS)
        return remote(
            turned.at[:, who, e, piece(e, g)],
            solved.at[:, sub, e, piece(e, g)],
            two_s.at[k - 1],
            two_r.at[k - 1, slot(e, g)],
            (slab, who),
        )

    def two_own(e, g):
        return pltpu.make_async_copy(
            turned.at[:, sub, e, piece(e, g)],
            solved.at[:, sub, e, piece(e, g)],
            two_o.at[slot(e, g)],
        )

    def two_send(e, g):
        for k in (2, 1, 3):
            two_copy(k, e, g).start()
        two_own(e, g).start()

    def two_wait(e, g):
        for k in range(1, SUBS):
            two_copy(k, e, g).wait_recv()
        two_own(e, g).wait()

    def ret_copy(g):
        return remote(
            ret.at[:, :, box_lanes(g)],
            back.at[:, :, box_lanes(g)],
            ret_s,
            ret_r.at[g],
            (ahead, sub),
        )

    def mate_copy(k):
        return remote(
            win.at[2 * k + 1],
            mate.at[k + odd],
            mate_s,
            mate_r.at[k],
            (partner, sub),
        )

    def ring(c):
        return pl.ds(c * RL, RL)

    def den_copy(j, c):
        return remote(
            win.at[2 * (HOPS + 1 - j), :, ring(c)],
            came.at[HOPS - j, :, ring(c)],
            den_s,
            den_r.at[j - 1, c],
            (ahead2, sub),
        )

    def fld_copy(j, c):
        return remote(
            fw.at[2 * j - 1, :, ring(c)],
            fw.at[2 * j + 1, :, ring(c)],
            fld_s,
            fld_r.at[j - 1, c],
            (behind2, sub),
        )

    def give_copy(j):
        return remote(
            fw.at[2 * j + 1],
            fw.at[2 * j + 2 * odd],
            give_s,
            give_r.at[j],
            (partner, sub),
        )

    start_x = []
    start_z = []
    for o in range(2):
        mine = slab * 2 + o
        start_x.append(lax.rem(corners[0, mine] - slab * SX + planes, planes))
        start_z.append(corners[1, mine])
    first, second, weight, shift_x, shift_z = [], [], [], [], []
    for s in range(2):
        i, j = pairs[s, 0], pairs[s, 1]
        first.append(lax.rem(i - 2 * slab + orbitals, orbitals))
        second.append(lax.rem(j - 2 * slab + orbitals, orbitals))
        half = planes // 2
        shift_x.append(lax.rem(corners[0, j] - corners[0, i] + half + planes, planes) - half)
        shift_z.append(corners[1, j] - corners[1, i])
        weight.append(jnp.where(count[0] > s, jnp.float32(1.0), jnp.float32(0.0)))

    row, col = iotas(LANES, GLANES)
    at = col - row - 32 * band(row)
    for o in range(2):
        put_z[o] = hot(at == start_z[o])
    row, col = iotas(REACH * SX, B)
    at = row - col
    for o in range(2):
        put_x[:, 2 * o * B : (2 * o + 2) * B] = twice(hot(at == start_x[o]))

    pl.semaphore_wait(barrier, 4 + SUBS - 1)
    load.wait()

    def send_boxes(g, _):
        box_copy(g).start()
        return 0

    lax.fori_loop(0, CHUNKS, send_boxes, 0)
    halo_copy(0).start()
    halo_copy(1).start()

    def deposit(g, _):
        parts = []
        for o in range(2):
            box = obx[o, :, own_lanes(g)]
            parts.append(pick1(box * box, put_z[o]))
        total = dot(put_x[...], jnp.concatenate(parts, axis=0))
        win[0:REACH, :, grid_lanes(g)] = total.reshape(REACH, SX, GLANES)
        return 0

    lax.fori_loop(0, CHUNKS, deposit, 0)

    def send_mate(k, _):
        mate_copy(HOPS - 1 - k).start()
        return 0

    lax.fori_loop(0, HOPS, send_mate, 0)

    row, col = iotas(LANES, LANES)
    same = band(row) == band(col)
    at = col - row
    for s in range(2):
        dz_to[s] = hot(same & (at == shift_z[s]))
        dz_from[s] = hot(same & (at == -shift_z[s]))
    row, col = iotas(B, B)
    at = row - col
    for s in range(2):
        dx_to[s] = twice(hot(at == shift_x[s]))
        dx_from[s] = twice(hot(at == -shift_x[s]))
    row, col = iotas(GLANES, LANES)
    at = row - col - 32 * band(col)
    for o in range(2):
        get_z[o] = hot(at == start_z[o])
    row, col = iotas(B, REACH * SX)
    at = col - row
    for o in range(2):
        get_x[o * B : (o + 1) * B, :] = twice(hot(at == start_x[o]))

    mate_copy(HOPS - 1).wait_recv()
    for c in range(RING):
        win[REACH, :, ring(c)] += mate[HOPS, :, ring(c)]
        den_copy(1, c).start()

    def density_step(j):
        m = HOPS + 1 - j
        mate_copy(HOPS - j).wait_recv()
        for c in range(RING):
            den_copy(j - 1, c).wait_recv()
            win[2 * m, :, ring(c)] += mate[m, :, ring(c)] + came[m, :, ring(c)]
            den_copy(j, c).start()

    halo_copy(0).wait_recv()
    halo_copy(1).wait_recv()
    keep_low = jnp.where(sub > 0, jnp.float32(1.0), jnp.float32(0.0))
    keep_high = jnp.where(sub < SUBS - 1, jnp.float32(1.0), jnp.float32(0.0))
    obx[:, :, 0:EDGE] = obx[:, :, 0:EDGE] * keep_low
    high_edge = EDGE + ROWS * B
    obx[:, :, high_edge : high_edge + EDGE] = obx[:, :, high_edge : high_edge + EDGE] * keep_high

    def forward(g, _):
        density_step(2 + g)
        parts = [split(obx[o, :, pl.ds(pl.multiple_of(g * LANES, 128), LANES + 2 * EDGE)]) for o in range(2)]
        beside = dot(
            jnp.concatenate([p[0] for p in parts] + [p[1] for p in parts], axis=0), near[...]
        )
        for o in range(2):
            inner = [p[:, EDGE : EDGE + LANES] for p in parts[o]]
            lap = dot(column[...], jnp.concatenate(inner, axis=0))
            lap = lap + beside[o * B : (o + 1) * B] + beside[(2 + o) * B : (3 + o) * B]
            out[o, :, box_lanes(g)] = -0.5 * lap
        box_copy(g).wait_recv()
        boxes = [obx[0, :, own_lanes(g)], obx[1, :, own_lanes(g)]]
        later = [nxt[0, :, box_lanes(g)], nxt[1, :, box_lanes(g)]]
        rhos = []
        for s in range(2):
            other = jnp.where(
                second[s] < 2,
                jnp.where(second[s] == 0, boxes[0], boxes[1]),
                jnp.where(second[s] == 2, later[0], later[1]),
            )
            shifted = dot(dx_to[s], pick1(other, dz_to[s]))
            moved[s, :, box_lanes(g)] = shifted
            rhos.append(jnp.where(first[s] == 0, boxes[0], boxes[1]) * shifted)
        wides = right3(rhos, wide_h[...], wide_l[...])
        for s in range(2):
            for k in range(0, GROUP, 2):
                two = left3(left[...], wides[s][:, k * GZ : (k + 2) * GZ])
                for m in range(2):
                    rows = pl.ds(pl.multiple_of((g * GROUP + k + m) * ROWS, 8), ROWS)
                    for q in range(SUBS):
                        spec[s, q, rows, :] = two[
                            q * ROWS : (q + 1) * ROWS, m * GZ : (m + 1) * GZ
                        ]
        for k in (2, 1, 3):
            one_copy(k, g).start()
        one_own(g).start()
        return 0

    lax.fori_loop(0, CHUNKS, forward, 0)
    density_step(HOPS)

    for c in range(RING):
        den_copy(HOPS, c).wait_recv()
        value = win[0, :, ring(c)] + mate[0, :, ring(c)] + came[0, :, ring(c)] + EPSILON
        root = jnp.exp(jnp.log(value) * (1.0 / 3.0))
        root = root - (root * root * root - value) / (3.0 * root * root)
        fw[1, :, ring(c)] = ext[:, ring(c)] - LOCAL_FACTOR * root
        fld_copy(1, c).start()
    give_copy(0).start()

    def field_last():
        for c in range(RING):
            fld_copy(HOPS, c).wait_recv()
        give_copy(HOPS).start()

    def field_step(j):
        for c in range(RING):
            fld_copy(j, c).wait_recv()
            fld_copy(j + 1, c).start()
        give_copy(j).start()

    def wait_one(g, _):
        for k in range(1, SUBS):
            one_copy(k, g).wait_recv()
        one_own(g).wait()
        return 0

    lax.fori_loop(0, CHUNKS, wait_one, 0)

    def along_y(e, t):
        a = 2 * t
        pieces = []
        for m in range(2):
            level = eigen[sub * ROWS + 8 * e + a + m]
            pieces.append((4.0 * math.pi) / (level_bc[...] + level))
        factor = jnp.concatenate(pieces, axis=1)
        for s in range(2):
            parts = []
            for m in range(2):
                parts.append(
                    jnp.concatenate(
                        [
                            pencil[s, q, pl.ds(8 * e + a + m, ROWS, stride=ROWS), :]
                            for q in range(SUBS)
                        ],
                        axis=0,
                    )
                )
            value = jnp.concatenate(parts, axis=1)
            value = left3(left[...], factor * left3(left[...], value))
            for m in range(2):
                for q in range(SUBS):
                    turned[s, q, e, pl.ds(a + m, ROWS, stride=8), :] = value[
                        q * ROWS : (q + 1) * ROWS, m * GZ : (m + 1) * GZ
                    ]

    def octet(e, _):
        def turn(t, _):
            along_y(e, t)
            return 0

        lax.fori_loop(0, 4, turn, 0)
        two_send(e, None)
        field_step(1 + e)
        return 0

    lax.fori_loop(0, OCTS - 1, octet, 0)

    def turn_last(t, _):
        along_y(OCTS - 1, t)
        return 0

    lax.fori_loop(0, 4, turn_last, 0)

    def send_two(g, _):
        two_send(OCTS - 1, g)
        return 0

    lax.fori_loop(0, CHUNKS, send_two, 0)
    for e in range(OCTS - 1):
        two_wait(e, None)

    def inverse(g, _):
        two_wait(OCTS - 1, g)
        boxes = [obx[0, :, own_lanes(g)], obx[1, :, own_lanes(g)]]
        mine = [None, None]
        theirs = [None, None]

        def add(held, k, value):
            held[k] = value if held[k] is None else held[k] + value

        wides = []
        for s in range(2):
            parts = []
            for k in range(0, GROUP, 2):
                pieces = []
                for m in range(2):
                    rows = pl.ds(pl.multiple_of((g * GROUP + k + m) * 8, 8), 8)
                    pieces.append(
                        jnp.concatenate(
                            [solved[s, q, e, rows, :] for q in range(SUBS) for e in range(OCTS)],
                            axis=0,
                        )
                    )
                parts.append(left3(left[...], jnp.concatenate(pieces, axis=1)))
            wides.append(jnp.concatenate(parts, axis=1))
        potentials = right3(wides, narrow_h[...], narrow_l[...])
        for s in range(2):
            potential = potentials[s] * (weight[s] * FOCK_SHARE)
            onto_first = potential * moved[s, :, box_lanes(g)]
            onto_second = dot(
                dx_from[s],
                pick1(potential * jnp.where(first[s] == 0, boxes[0], boxes[1]), dz_from[s]),
            )
            for k in range(2):
                add(mine, k, jnp.where(first[s] == k, onto_first, 0.0))
                add(mine, k, jnp.where(second[s] == k, onto_second, 0.0))
                add(theirs, k, jnp.where(second[s] == 2 + k, onto_second, 0.0))
        for k in range(2):
            out[k, :, box_lanes(g)] -= mine[k]
            ret[k, :, box_lanes(g)] = theirs[k]
        ret_copy(g).start()
        return 0

    def inverse_step(g, _):
        field_step(OCTS + g)
        return inverse(g, _)

    lax.fori_loop(0, CHUNKS - 1, inverse_step, 0)
    field_last()
    inverse(CHUNKS - 1, 0)

    def wait_give(j, _):
        give_copy(j).wait_recv()
        return 0

    lax.fori_loop(0, HOPS + 1, wait_give, 0)

    def finish(g, _):
        field = fw[1 : REACH + 1, :, grid_lanes(g)].reshape(REACH * SX, GLANES)
        local = dot(get_x[...], stack(field))
        ret_copy(g).wait_recv()
        for o in range(2):
            here = right1(local[o * B : (o + 1) * B], get_z[o])
            out[o, :, box_lanes(g)] += (
                here * obx[o, :, own_lanes(g)] - back[o, :, box_lanes(g)]
            )
        return 0

    lax.fori_loop(0, CHUNKS, finish, 0)

    remote(obx.at[:, :, EDGE : EDGE + ROWS * B], nxt, box_s, box_r.at[0], (behind, sub)).wait_send()
    remote(ret, back, ret_s, ret_r.at[0], (ahead, sub)).wait_send()
    for k in range(1, SUBS):
        who = lax.rem(sub + k, SUBS)
        remote(spec.at[:, who], pencil.at[:, sub], one_s.at[k - 1], one_r.at[0, 0], (slab, who)).wait_send()
        remote(turned.at[:, who], solved.at[:, sub], two_s.at[k - 1], two_r.at[0, 0], (slab, who)).wait_send()
    halo_copy(0).wait_send()
    halo_copy(1).wait_send()
    eight = win.at[0:HOPS]
    nine = win.at[0 : HOPS + 1]
    remote(eight, came, mate_s, mate_r.at[0], (partner, sub)).wait_send()
    remote(eight, came, den_s, den_r.at[0, 0], (ahead2, sub)).wait_send()
    remote(eight, came, fld_s, fld_r.at[0, 0], (behind2, sub)).wait_send()
    remote(nine, mate, give_s, give_r.at[0], (partner, sub)).wait_send()


def local(slabs, orbitals, external_potential, corners, pair_list, pair_count):
    vmem = pl.BlockSpec(memory_space=pltpu.VMEM)
    smem = pl.BlockSpec(memory_space=pltpu.SMEM)
    table = tables()
    arrays = [jnp.asarray(t) for t in table[:-1]]
    eigen = jnp.asarray(table[-1])
    dma = pltpu.SemaphoreType.DMA
    part = (2, B, ROWS * B)
    turns = (2, SUBS, ROWS * ROWS, GZ)
    octs = (2, SUBS, OCTS, ROWS * 8, GZ)
    block = (SX, ROWS * GZ)
    return pl.pallas_call(
        functools.partial(kernel, slabs),
        out_shape=jax.ShapeDtypeStruct(orbitals.shape, F32),
        in_specs=[smem] * 4 + [pl.BlockSpec(memory_space=pl.ANY)] + [vmem] * (1 + len(arrays)),
        out_specs=vmem,
        scratch_shapes=[
            pltpu.VMEM((2, B, ROWS * B + 2 * EDGE), F32),
            pltpu.VMEM(part, F32),
            pltpu.VMEM(part, F32),
            pltpu.VMEM(turns, F32),
            pltpu.VMEM(turns, F32),
            pltpu.VMEM(octs, F32),
            pltpu.VMEM(octs, F32),
            pltpu.VMEM((REACH + 1,) + block, F32),
            pltpu.VMEM((HOPS + 1,) + block, F32),
            pltpu.VMEM((HOPS,) + block, F32),
            pltpu.VMEM((REACH + 3,) + block, F32),
            pltpu.VMEM(part, F32),
            pltpu.VMEM(part, F32),
            pltpu.VMEM((2, LANES, LANES), BF16),
            pltpu.VMEM((2, LANES, LANES), BF16),
            pltpu.VMEM((2, B, 2 * B), BF16),
            pltpu.VMEM((2, B, 2 * B), BF16),
            pltpu.VMEM((2, LANES, GLANES), BF16),
            pltpu.VMEM((2, GLANES, LANES), BF16),
            pltpu.VMEM((REACH * SX, 4 * B), BF16),
            pltpu.VMEM((2 * B, 2 * REACH * SX), BF16),
            dma,
            dma,
            dma((CHUNKS,)),
            dma((2,)),
            dma((2,)),
            dma((SUBS - 1,)),
            dma((SUBS - 1, CHUNKS)),
            dma((CHUNKS,)),
            dma((SUBS - 1,)),
            dma((SUBS - 1, OCTS - 1 + CHUNKS)),
            dma((OCTS - 1 + CHUNKS,)),
            dma,
            dma((CHUNKS,)),
            dma,
            dma((HOPS,)),
            dma,
            dma((HOPS, RING)),
            dma,
            dma((HOPS, RING)),
            dma,
            dma((HOPS + 1,)),
        ],
        compiler_params=pltpu.CompilerParams(
            collective_id=0, has_side_effects=True, vmem_limit_bytes=60 * 1024 * 1024
        ),
        name="orbitals",
    )(corners.T, pair_list, pair_count, eigen, orbitals, external_potential, *arrays)


def solution(mesh):
    placed = (P("slab", None, "sub"), P("slab", "sub"), P(), P("slab", None), P("slab"))
    return jax.shard_map(
        functools.partial(local, mesh.shape["slab"]),
        mesh=mesh,
        in_specs=placed,
        out_specs=P("slab", None, "sub"),
        check_vma=False,
    )
```

```python
import functools
import math

import jax
import jax.numpy as jnp
import ml_dtypes
import numpy as np
from jax import lax
from jax.experimental import pallas as pl
from jax.experimental.pallas import tpu as pltpu
from jax.sharding import PartitionSpec as P

SCREEN = 0.0008
FOCK_SHARE = 0.25
LOCAL_FACTOR = (3.0 / math.pi) ** (1.0 / 3.0)
EPSILON = 1e-06

B = 96
ROWS = 24
GZ = 128
SX = 8
REACH = 16
SUBS = 4
GROUP = 4
CHUNKS = ROWS // GROUP
LANES = GROUP * B
GLANES = GROUP * GZ
EDGE = 128
RING = 3
RL = ROWS * GZ // RING
HOPS = REACH // 2
PACK = LANES // 128
SLICE = PACK * ROWS

F32 = jnp.float32
BF16 = jnp.bfloat16
MESH = pl.DeviceIdType.MESH


def halves(value):
    high = value.astype(ml_dtypes.bfloat16)
    low = (value - high.astype(np.float64)).astype(ml_dtypes.bfloat16)
    return high, low


def tables():
    level = np.arange(B, dtype=np.float64) + 1.0
    sine = math.sqrt(2.0 / (B + 1)) * np.sin(math.pi * level[:, None] * level[None, :] / (B + 1))
    eigen = 2.0 - 2.0 * np.cos(math.pi * level / (B + 1))
    high, low = halves(sine)
    left = np.block([[high, high], [low, np.zeros_like(low)]])
    wide = np.zeros((LANES, LANES), np.float64)
    for k in range(GROUP):
        lane = np.arange(B)
        place = k * 128 + lane if k < PACK else (lane // 32) * 128 + B + lane % 32
        wide[k * B : (k + 1) * B, place] = sine
    order = np.array([q * ROWS + GROUP * g + k for k in range(GROUP) for q in range(SUBS) for g in range(CHUNKS)])
    zero = np.zeros_like(low)
    into = np.block([[high[:, order], high[:, order]], [low[:, order], zero]])
    outof = np.block([[high[order], high[order]], [low[order], zero]])
    wide_high, wide_low = halves(wide)
    narrow_high, narrow_low = wide_high.T.copy(), wide_low.T.copy()
    rows = np.arange(LANES + 2 * EDGE)[:, None] - EDGE
    cols = np.arange(LANES)[None, :]
    beside = np.abs(rows - cols)
    near = (beside == B) | ((beside == 1) & (rows // B == cols // B))
    near = near.astype(ml_dtypes.bfloat16)
    line = np.abs(np.arange(B)[:, None] - np.arange(B)[None, :])
    column = ((line == 1) * 1.0 - (line == 0) * 6.0).astype(ml_dtypes.bfloat16)
    column = np.concatenate([column, column], axis=1)
    level_bc = np.ones((B, GZ), np.float64)
    level_bc[:, :B] = eigen[:, None] + eigen[None, :] + SCREEN
    return (
        left,
        into,
        outof,
        wide_high,
        wide_low,
        narrow_high,
        narrow_low,
        near,
        column,
        level_bc.astype(np.float32),
        eigen.astype(np.float32),
    )


def split(value):
    high = value.astype(BF16)
    low = (value - high.astype(F32)).astype(BF16)
    return high, low


def stack(value):
    return jnp.concatenate(split(value), axis=0)


def dot(a, b):
    return jnp.dot(a, b, preferred_element_type=F32)


def left3(table, value):
    both = dot(table, stack(value))
    return both[:B] + both[B:]


def right3(values, t_high, t_low):
    parts = [split(v) for v in values]
    rows = values[0].shape[0]
    count = len(values)
    high = jnp.concatenate([p[0] for p in parts], axis=0)
    full = dot(jnp.concatenate([high] + [p[1] for p in parts], axis=0), t_high)
    rest = dot(high, t_low)
    return [
        full[k * rows : (k + 1) * rows]
        + full[(count + k) * rows : (count + k + 1) * rows]
        + rest[k * rows : (k + 1) * rows]
        for k in range(count)
    ]


def right1(value, table):
    rows = value.shape[0]
    both = dot(stack(value), table)
    return both[:rows] + both[rows:]


def pick1(value, table):
    return dot(stack(value), table).astype(BF16)


def iotas(rows, cols):
    return (
        lax.broadcasted_iota(jnp.int32, (rows, cols), 0),
        lax.broadcasted_iota(jnp.int32, (rows, cols), 1),
    )


def band(index):
    one = jnp.int32(1)
    zero = jnp.int32(0)
    total = jnp.zeros_like(index)
    for k in range(1, GROUP):
        total = total + jnp.where(index >= k * B, one, zero)
    return total


def hot(condition):
    return jnp.where(condition, 1.0, 0.0).astype(BF16)


def twice(table):
    return jnp.concatenate([table, table], axis=1)


def kernel(
    slabs,
    corners,
    pairs,
    count,
    eigen,
    orb,
    ext,
    left,
    into,
    outof,
    wide_h,
    wide_l,
    narrow_h,
    narrow_l,
    near,
    column,
    level_bc,
    out,
    obx,
    nxt,
    moved,
    spec,
    pencil,
    turned,
    solved,
    win,
    mate,
    came,
    fw,
    ret,
    back,
    flag,
    told,
    dz_to,
    dz_from,
    dx_to,
    dx_from,
    put_z,
    get_z,
    put_x,
    get_x,
    load_sem,
    box_s,
    box_r,
    halo_s,
    halo_r,
    one_s,
    one_r,
    one_o,
    two_s,
    two_r,
    two_o,
    ret_s,
    ret_r,
    flag_s,
    flag_r,
    mate_s,
    mate_r,
    den_s,
    den_r,
    fld_s,
    fld_r,
    give_s,
    give_r,
):
    slab = lax.axis_index("slab")
    sub = lax.axis_index("sub")
    ahead = lax.rem(slab + 1, slabs)
    behind = lax.rem(slab + slabs - 1, slabs)
    ahead2 = lax.rem(slab + 2, slabs)
    behind2 = lax.rem(slab + slabs - 2, slabs)
    odd = lax.rem(slab, 2)
    partner = slab + 1 - 2 * odd
    planes = slabs * SX
    orbitals = 2 * slabs

    load = pltpu.make_async_copy(orb, obx.at[:, :, EDGE : EDGE + ROWS * B], load_sem)
    load.start()
    mate[0] = jnp.zeros((SX, ROWS * GZ), F32)
    mate[HOPS] = jnp.zeros((SX, ROWS * GZ), F32)
    win[REACH] = jnp.zeros((SX, ROWS * GZ), F32)
    barrier = pltpu.get_barrier_semaphore()
    for who in (ahead, behind, ahead2, behind2):
        pl.semaphore_signal(barrier, inc=1, device_id=(who, sub), device_id_type=MESH)
    for k in range(1, SUBS):
        pl.semaphore_signal(
            barrier, inc=1, device_id=(slab, lax.rem(sub + k, SUBS)), device_id_type=MESH
        )

    def remote(src, dst, send, recv, who):
        return pltpu.make_async_remote_copy(
            src_ref=src,
            dst_ref=dst,
            send_sem=send,
            recv_sem=recv,
            device_id=who,
            device_id_type=MESH,
        )

    def box_lanes(g):
        return pl.ds(pl.multiple_of(g * LANES, 128), LANES)

    def own_lanes(g):
        return pl.ds(pl.multiple_of(EDGE + g * LANES, 128), LANES)

    def grid_lanes(g):
        return pl.ds(pl.multiple_of(g * GLANES, 128), GLANES)

    def box_copy(g):
        return remote(
            orb.at[:, :, box_lanes(g)],
            nxt.at[:, :, box_lanes(g)],
            box_s,
            box_r.at[g],
            (behind, sub),
        )

    def halo_copy(side):
        start = EDGE if side == 0 else ROWS * B
        land = EDGE + ROWS * B if side == 0 else 0
        who = lax.rem(sub + (SUBS - 1 if side == 0 else 1), SUBS)
        return remote(
            obx.at[:, :, start : start + EDGE],
            obx.at[:, :, land : land + EDGE],
            halo_s.at[side],
            halo_r.at[side],
            (slab, who),
        )

    def spec_rows(g):
        return pl.ds(pl.multiple_of(g * SLICE, 8), SLICE)

    def pencil_rows(g):
        return pl.ds(pl.multiple_of((sub * CHUNKS + g) * SLICE, 8), SLICE)

    def one_copy(k, s, g):
        who = lax.rem(sub + k, SUBS)
        return remote(
            spec.at[s, who, spec_rows(g)],
            pencil.at[s, pencil_rows(g)],
            one_s.at[k - 1],
            one_r.at[k - 1, s, g],
            (slab, who),
        )

    def one_own(s, g):
        return pltpu.make_async_copy(
            spec.at[s, sub, spec_rows(g)], pencil.at[s, pencil_rows(g)], one_o.at[s, g]
        )

    def turned_rows(who, g):
        return pl.ds(pl.multiple_of((who * CHUNKS + g) * SLICE, 8), SLICE)

    def two_copy(k, s, g):
        who = lax.rem(sub + k, SUBS)
        return remote(
            turned.at[s, turned_rows(who, g)],
            solved.at[s, sub, spec_rows(g)],
            two_s.at[k - 1],
            two_r.at[k - 1, s, g],
            (slab, who),
        )

    def two_own(s, g):
        return pltpu.make_async_copy(
            turned.at[s, turned_rows(sub, g)], solved.at[s, sub, spec_rows(g)], two_o.at[s, g]
        )

    def ret_copy(s, g):
        return remote(
            ret.at[s, :, box_lanes(g)],
            back.at[s, :, box_lanes(g)],
            ret_s,
            ret_r.at[s, g],
            (ahead, sub),
        )

    def flag_copy():
        return remote(flag, told, flag_s, flag_r, (ahead, sub))

    def mate_copy(k):
        return remote(
            win.at[2 * k + 1],
            mate.at[k + odd],
            mate_s,
            mate_r.at[k],
            (partner, sub),
        )

    def ring(c):
        return pl.ds(c * RL, RL)

    def den_copy(j, c):
        return remote(
            win.at[2 * (HOPS + 1 - j), :, ring(c)],
            came.at[HOPS - j, :, ring(c)],
            den_s,
            den_r.at[j - 1, c],
            (ahead2, sub),
        )

    def fld_copy(j, c):
        return remote(
            fw.at[2 * j - 1, :, ring(c)],
            fw.at[2 * j + 1, :, ring(c)],
            fld_s,
            fld_r.at[j - 1, c],
            (behind2, sub),
        )

    def give_copy(j):
        return remote(
            fw.at[2 * j + 1],
            fw.at[2 * j + 2 * odd],
            give_s,
            give_r.at[j],
            (partner, sub),
        )

    start_x = []
    start_z = []
    for o in range(2):
        mine = slab * 2 + o
        start_x.append(lax.rem(corners[0, mine] - slab * SX + planes, planes))
        start_z.append(corners[1, mine])
    first, second, weight, shift_x, shift_z = [], [], [], [], []
    for s in range(2):
        i, j = pairs[s, 0], pairs[s, 1]
        first.append(lax.rem(i - 2 * slab + orbitals, orbitals))
        second.append(lax.rem(j - 2 * slab + orbitals, orbitals))
        half = planes // 2
        shift_x.append(lax.rem(corners[0, j] - corners[0, i] + half + planes, planes) - half)
        shift_z.append(corners[1, j] - corners[1, i])
        weight.append(jnp.where(count[0] > s, jnp.float32(1.0), jnp.float32(0.0)))

    pl.semaphore_wait(barrier, 4 + SUBS - 1)

    def send_boxes(g, _):
        box_copy(g).start()
        return 0

    lax.fori_loop(0, CHUNKS, send_boxes, 0)
    for s in range(2):
        for k in range(2):
            mark = jnp.where(second[s] == 2 + k, jnp.float32(1.0), jnp.float32(0.0))
            flag[s, k] = jnp.zeros((8, 128), F32) + mark
    flag_copy().start()

    row, col = iotas(LANES, GLANES)
    at = col - row - 32 * band(row)
    for o in range(2):
        put_z[o] = hot(at == start_z[o])
    row, col = iotas(REACH * SX, B)
    at = row - col
    for o in range(2):
        put_x[:, 2 * o * B : (2 * o + 2) * B] = twice(hot(at == start_x[o]))

    load.wait()
    halo_copy(0).start()
    halo_copy(1).start()

    def deposit(g, _):
        parts = []
        for o in range(2):
            box = obx[o, :, own_lanes(g)]
            parts.append(pick1(box * box, put_z[o]))
        total = dot(put_x[...], jnp.concatenate(parts, axis=0))
        win[0:REACH, :, grid_lanes(g)] = total.reshape(REACH, SX, GLANES)
        return 0

    lax.fori_loop(0, CHUNKS, deposit, 0)

    def send_mate(k, _):
        mate_copy(HOPS - 1 - k).start()
        return 0

    lax.fori_loop(0, HOPS, send_mate, 0)

    row, col = iotas(LANES, LANES)
    same = band(row) == band(col)
    at = col - row
    for s in range(2):
        dz_to[s] = hot(same & (at == shift_z[s]))
    row, col = iotas(B, B)
    at = row - col
    for s in range(2):
        dx_to[s] = twice(hot(at == shift_x[s]))

    mate_copy(HOPS - 1).wait_recv()
    for c in range(RING):
        win[REACH, :, ring(c)] += mate[HOPS, :, ring(c)]
        den_copy(1, c).start()

    def density_step(j):
        m = HOPS + 1 - j
        mate_copy(HOPS - j).wait_recv()
        for c in range(RING):
            den_copy(j - 1, c).wait_recv()
            win[2 * m, :, ring(c)] += mate[m, :, ring(c)] + came[m, :, ring(c)]
            den_copy(j, c).start()

    halo_copy(0).wait_recv()
    halo_copy(1).wait_recv()
    keep_low = jnp.where(sub > 0, jnp.float32(1.0), jnp.float32(0.0))
    keep_high = jnp.where(sub < SUBS - 1, jnp.float32(1.0), jnp.float32(0.0))
    obx[:, :, 0:EDGE] = obx[:, :, 0:EDGE] * keep_low
    high_edge = EDGE + ROWS * B
    obx[:, :, high_edge : high_edge + EDGE] = obx[:, :, high_edge : high_edge + EDGE] * keep_high

    def forward(g, _):
        density_step(2 + g)
        parts = [split(obx[o, :, pl.ds(pl.multiple_of(g * LANES, 128), LANES + 2 * EDGE)]) for o in range(2)]
        beside = dot(
            jnp.concatenate([p[0] for p in parts] + [p[1] for p in parts], axis=0), near[...]
        )
        for o in range(2):
            inner = [p[:, EDGE : EDGE + LANES] for p in parts[o]]
            lap = dot(column[...], jnp.concatenate(inner, axis=0))
            lap = lap + beside[o * B : (o + 1) * B] + beside[(2 + o) * B : (3 + o) * B]
            out[o, :, box_lanes(g)] = -0.5 * lap
        box_copy(g).wait_recv()
        boxes = [obx[0, :, own_lanes(g)], obx[1, :, own_lanes(g)]]
        later = [nxt[0, :, box_lanes(g)], nxt[1, :, box_lanes(g)]]
        rhos = []
        for s in range(2):
            other = jnp.where(
                second[s] < 2,
                jnp.where(second[s] == 0, boxes[0], boxes[1]),
                jnp.where(second[s] == 2, later[0], later[1]),
            )
            shifted = dot(dx_to[s], pick1(other, dz_to[s]))
            moved[s, :, box_lanes(g)] = shifted
            rhos.append(jnp.where(first[s] == 0, boxes[0], boxes[1]) * shifted)
        wides = right3(rhos, wide_h[...], wide_l[...])
        for s in range(2):
            both = left3(left[...], wides[s])
            for m in range(PACK):
                rows = pl.ds(pl.multiple_of((g * PACK + m) * ROWS, 8), ROWS)
                for q in range(SUBS):
                    spec[s, q, rows, :] = both[q * ROWS : (q + 1) * ROWS, m * 128 : (m + 1) * 128]
            for k in (2, 1, 3):
                one_copy(k, s, g).start()
            one_own(s, g).start()
        return 0

    lax.fori_loop(0, CHUNKS, forward, 0)
    density_step(HOPS)

    for c in range(RING):
        den_copy(HOPS, c).wait_recv()
        value = win[0, :, ring(c)] + mate[0, :, ring(c)] + came[0, :, ring(c)] + EPSILON
        root = jnp.exp(jnp.log(value) * (1.0 / 3.0))
        root = root - (root * root * root - value) / (3.0 * root * root)
        fw[1, :, ring(c)] = ext[:, ring(c)] - LOCAL_FACTOR * root
        fld_copy(1, c).start()
    give_copy(0).start()

    def field_last():
        for c in range(RING):
            fld_copy(HOPS, c).wait_recv()
        give_copy(HOPS).start()

    def field_step(j):
        for c in range(RING):
            fld_copy(j, c).wait_recv()
            fld_copy(j + 1, c).start()
        give_copy(j).start()

    row, col = iotas(LANES, LANES)
    same = band(row) == band(col)
    at = col - row
    for s in range(2):
        dz_from[s] = hot(same & (at == -shift_z[s]))
    row, col = iotas(B, B)
    at = row - col
    for s in range(2):
        dx_from[s] = twice(hot(at == -shift_x[s]))
    row, col = iotas(GLANES, LANES)
    at = row - col - 32 * band(col)
    for o in range(2):
        get_z[o] = hot(at == start_z[o])
    row, col = iotas(B, REACH * SX)
    at = col - row
    for o in range(2):
        get_x[o * B : (o + 1) * B, :] = twice(hot(at == start_x[o]))
    lane = lax.broadcasted_iota(jnp.int32, (ROWS, 128), 1)

    def along_y(s, t):
        a = 2 * t
        pieces, values = [], []
        for m in range(2):
            level = eigen[sub * ROWS + a + m]
            pieces.append((4.0 * math.pi) / (level_bc[...] + level))
            tiles = [
                pencil[s, pl.ds(k * ROWS + a + m, SUBS * CHUNKS, stride=SLICE), :]
                for k in range(PACK)
            ]
            last = [pltpu.roll(tiles[k], 32 * (k + 1), 1) for k in range(PACK)]
            rest = jnp.where(lane < 32, last[0], jnp.where(lane < 64, last[1], last[2]))
            values.append(jnp.concatenate(tiles + [rest], axis=0))
        factor = jnp.concatenate(pieces, axis=1)
        value = left3(into[...], jnp.concatenate(values, axis=1))
        value = left3(outof[...], factor * value)
        for m in range(2):
            tile = value[:, m * 128 : (m + 1) * 128]
            rest = tile[PACK * ROWS :]
            for k in range(PACK):
                packed = jnp.where(
                    lane < B, tile[k * ROWS : (k + 1) * ROWS], pltpu.roll(rest, B - 32 * k, 1)
                )
                turned[s, pl.ds(k * ROWS + a + m, SUBS * CHUNKS, stride=SLICE), :] = packed

    def middle(s):
        def wait_one(g, _):
            for k in range(1, SUBS):
                one_copy(k, s, g).wait_recv()
            one_own(s, g).wait()
            return 0

        def turn(t, _):
            along_y(s, t)
            return 0

        def send_two(g, _):
            for k in (2, 1, 3):
                two_copy(k, s, g).start()
            two_own(s, g).start()
            return 0

        lax.fori_loop(0, CHUNKS, wait_one, 0)
        lax.fori_loop(0, ROWS // 2, turn, 0)
        lax.fori_loop(0, CHUNKS, send_two, 0)

    middle(0)
    field_step(1)
    middle(1)

    def inverse(s, g):
        for k in range(1, SUBS):
            two_copy(k, s, g).wait_recv()
        two_own(s, g).wait()
        pieces = []
        for m in range(PACK):
            rows = pl.ds(pl.multiple_of((g * PACK + m) * ROWS, 8), ROWS)
            pieces.append(jnp.concatenate([solved[s, q, rows, :] for q in range(SUBS)], axis=0))
        spread = left3(left[...], jnp.concatenate(pieces, axis=1))
        potential = right3([spread], narrow_h[...], narrow_l[...])[0]
        potential = potential * (weight[s] * FOCK_SHARE)
        onto_first = potential * moved[s, :, box_lanes(g)]
        box = jnp.where(first[s] == 0, obx[0, :, own_lanes(g)], obx[1, :, own_lanes(g)])
        onto_second = dot(dx_from[s], pick1(potential * box, dz_from[s]))
        ret[s, :, box_lanes(g)] = onto_second
        ret_copy(s, g).start()
        for k in range(2):
            out[k, :, box_lanes(g)] -= jnp.where(first[s] == k, onto_first, 0.0) + jnp.where(
                second[s] == k, onto_second, 0.0
            )

    def inverse_first(g, _):
        inverse(0, g)
        field_step(2 + g)
        return 0

    def inverse_second(g, _):
        inverse(1, g)
        return 0

    lax.fori_loop(0, CHUNKS, inverse_first, 0)
    field_last()
    lax.fori_loop(0, CHUNKS, inverse_second, 0)
    flag_copy().wait_recv()

    def wait_give(j, _):
        give_copy(j).wait_recv()
        return 0

    lax.fori_loop(0, HOPS + 1, wait_give, 0)

    def finish(g, _):
        field = fw[1 : REACH + 1, :, grid_lanes(g)].reshape(REACH * SX, GLANES)
        local = dot(get_x[...], stack(field))
        for s in range(2):
            ret_copy(s, g).wait_recv()
        came_back = [back[s, :, box_lanes(g)] for s in range(2)]
        for o in range(2):
            here = right1(local[o * B : (o + 1) * B], get_z[o])
            total = here * obx[o, :, own_lanes(g)]
            for s in range(2):
                marks = jnp.concatenate([told[s, o]] * (LANES // 128), axis=1)
                marks = jnp.concatenate([marks] * (B // 8), axis=0)
                total = total - marks * came_back[s]
            out[o, :, box_lanes(g)] += total
        return 0

    lax.fori_loop(0, CHUNKS, finish, 0)

    remote(orb, nxt, box_s, box_r.at[0], (behind, sub)).wait_send()
    remote(ret, back, ret_s, ret_r.at[0, 0], (ahead, sub)).wait_send()
    flag_copy().wait_send()
    for k in range(1, SUBS):
        who = lax.rem(sub + k, SUBS)
        whole = solved.at[:, 0]
        remote(whole, whole, one_s.at[k - 1], one_r.at[0, 0, 0], (slab, who)).wait_send()
        remote(whole, whole, two_s.at[k - 1], two_r.at[0, 0, 0], (slab, who)).wait_send()
    halo_copy(0).wait_send()
    halo_copy(1).wait_send()
    eight = win.at[0:HOPS]
    nine = win.at[0 : HOPS + 1]
    remote(eight, came, mate_s, mate_r.at[0], (partner, sub)).wait_send()
    remote(eight, came, den_s, den_r.at[0, 0], (ahead2, sub)).wait_send()
    remote(eight, came, fld_s, fld_r.at[0, 0], (behind2, sub)).wait_send()
    remote(nine, mate, give_s, give_r.at[0], (partner, sub)).wait_send()


def local(slabs, orbitals, external_potential, corners, pair_list, pair_count):
    vmem = pl.BlockSpec(memory_space=pltpu.VMEM)
    smem = pl.BlockSpec(memory_space=pltpu.SMEM)
    table = tables()
    arrays = [jnp.asarray(t) for t in table[:-1]]
    eigen = jnp.asarray(table[-1])
    dma = pltpu.SemaphoreType.DMA
    part = (2, B, ROWS * B)
    parted = (2, SUBS, CHUNKS * SLICE, 128)
    joined = (2, SUBS * CHUNKS * SLICE, 128)
    block = (SX, ROWS * GZ)
    return pl.pallas_call(
        functools.partial(kernel, slabs),
        out_shape=jax.ShapeDtypeStruct(orbitals.shape, F32),
        in_specs=[smem] * 4 + [pl.BlockSpec(memory_space=pl.ANY)] + [vmem] * (1 + len(arrays)),
        out_specs=vmem,
        scratch_shapes=[
            pltpu.VMEM((2, B, ROWS * B + 2 * EDGE), F32),
            pltpu.VMEM(part, F32),
            pltpu.VMEM(part, F32),
            pltpu.VMEM(parted, F32),
            pltpu.VMEM(joined, F32),
            pltpu.VMEM(joined, F32),
            pltpu.VMEM(parted, F32),
            pltpu.VMEM((REACH + 1,) + block, F32),
            pltpu.VMEM((HOPS + 1,) + block, F32),
            pltpu.VMEM((HOPS,) + block, F32),
            pltpu.VMEM((REACH + 3,) + block, F32),
            pltpu.VMEM(part, F32),
            pltpu.VMEM(part, F32),
            pltpu.VMEM((2, 2, 8, 128), F32),
            pltpu.VMEM((2, 2, 8, 128), F32),
            pltpu.VMEM((2, LANES, LANES), BF16),
            pltpu.VMEM((2, LANES, LANES), BF16),
            pltpu.VMEM((2, B, 2 * B), BF16),
            pltpu.VMEM((2, B, 2 * B), BF16),
            pltpu.VMEM((2, LANES, GLANES), BF16),
            pltpu.VMEM((2, GLANES, LANES), BF16),
            pltpu.VMEM((REACH * SX, 4 * B), BF16),
            pltpu.VMEM((2 * B, 2 * REACH * SX), BF16),
            dma,
            dma,
            dma((CHUNKS,)),
            dma((2,)),
            dma((2,)),
            dma((SUBS - 1,)),
            dma((SUBS - 1, 2, CHUNKS)),
            dma((2, CHUNKS)),
            dma((SUBS - 1,)),
            dma((SUBS - 1, 2, CHUNKS)),
            dma((2, CHUNKS)),
            dma,
            dma((2, CHUNKS)),
            dma,
            dma,
            dma,
            dma((HOPS,)),
            dma,
            dma((HOPS, RING)),
            dma,
            dma((HOPS, RING)),
            dma,
            dma((HOPS + 1,)),
        ],
        compiler_params=pltpu.CompilerParams(
            collective_id=0, has_side_effects=True, vmem_limit_bytes=60 * 1024 * 1024
        ),
        name="orbitals",
    )(corners.T, pair_list, pair_count, eigen, orbitals, external_potential, *arrays)


def solution(mesh):
    placed = (P("slab", None, "sub"), P("slab", "sub"), P(), P("slab", None), P("slab"))
    return jax.shard_map(
        functools.partial(local, mesh.shape["slab"]),
        mesh=mesh,
        in_specs=placed,
        out_specs=P("slab", None, "sub"),
        check_vma=False,
    )
```

```python
import functools
import math

import jax
import jax.numpy as jnp
import ml_dtypes
import numpy as np
from jax import lax
from jax.experimental import pallas as pl
from jax.experimental.pallas import tpu as pltpu
from jax.sharding import PartitionSpec as P

SCREEN = 0.0008
FOCK_SHARE = 0.25
LOCAL_FACTOR = (3.0 / math.pi) ** (1.0 / 3.0)
EPSILON = 1e-06

B = 96
ROWS = 24
GZ = 128
SX = 8
REACH = 16
SUBS = 4
GROUP = 4
CHUNKS = ROWS // GROUP
LANES = GROUP * B
GLANES = GROUP * GZ
EDGE = 128
RING = 3
RL = ROWS * GZ // RING
HOPS = REACH // 2
PACK = LANES // 128
SLICE = PACK * ROWS

F32 = jnp.float32
BF16 = jnp.bfloat16
MESH = pl.DeviceIdType.MESH


def halves(value):
    high = value.astype(ml_dtypes.bfloat16)
    low = (value - high.astype(np.float64)).astype(ml_dtypes.bfloat16)
    return high, low


def tables():
    level = np.arange(B, dtype=np.float64) + 1.0
    sine = math.sqrt(2.0 / (B + 1)) * np.sin(math.pi * level[:, None] * level[None, :] / (B + 1))
    eigen = 2.0 - 2.0 * np.cos(math.pi * level / (B + 1))
    high, low = halves(sine)
    left = np.block([[high, high], [low, np.zeros_like(low)]])
    wide = np.zeros((LANES, LANES), np.float64)
    for k in range(GROUP):
        lane = np.arange(B)
        place = k * 128 + lane if k < PACK else (lane // 32) * 128 + B + lane % 32
        wide[k * B : (k + 1) * B, place] = sine
    order = np.array([q * ROWS + GROUP * g + k for k in range(GROUP) for q in range(SUBS) for g in range(CHUNKS)])
    zero = np.zeros_like(low)
    into = np.block([[high[:, order], high[:, order]], [low[:, order], zero]])
    outof = np.block([[high[order], high[order]], [low[order], zero]])
    wide_high, wide_low = halves(wide)
    narrow_high, narrow_low = wide_high.T.copy(), wide_low.T.copy()
    rows = np.arange(LANES + 2 * EDGE)[:, None] - EDGE
    cols = np.arange(LANES)[None, :]
    beside = np.abs(rows - cols)
    near = (beside == B) | ((beside == 1) & (rows // B == cols // B))
    near = near.astype(ml_dtypes.bfloat16)
    line = np.abs(np.arange(B)[:, None] - np.arange(B)[None, :])
    column = ((line == 1) * 1.0 - (line == 0) * 6.0).astype(ml_dtypes.bfloat16)
    column = np.concatenate([column, column], axis=1)
    level_bc = np.ones((B, GZ), np.float64)
    level_bc[:, :B] = eigen[:, None] + eigen[None, :] + SCREEN
    return (
        left,
        into,
        outof,
        wide_high,
        wide_low,
        narrow_high,
        narrow_low,
        near,
        column,
        level_bc.astype(np.float32),
        eigen.astype(np.float32),
    )


def split(value):
    high = value.astype(BF16)
    low = (value - high.astype(F32)).astype(BF16)
    return high, low


def stack(value):
    return jnp.concatenate(split(value), axis=0)


def dot(a, b):
    return jnp.dot(a, b, preferred_element_type=F32)


def left3(table, value):
    both = dot(table, stack(value))
    return both[:B] + both[B:]


def right3(values, t_high, t_low):
    parts = [split(v) for v in values]
    rows = values[0].shape[0]
    count = len(values)
    high = jnp.concatenate([p[0] for p in parts], axis=0)
    full = dot(jnp.concatenate([high] + [p[1] for p in parts], axis=0), t_high)
    rest = dot(high, t_low)
    return [
        full[k * rows : (k + 1) * rows]
        + full[(count + k) * rows : (count + k + 1) * rows]
        + rest[k * rows : (k + 1) * rows]
        for k in range(count)
    ]


def right1(value, table):
    rows = value.shape[0]
    both = dot(stack(value), table)
    return both[:rows] + both[rows:]


def pick1(value, table):
    return dot(stack(value), table).astype(BF16)


def iotas(rows, cols):
    return (
        lax.broadcasted_iota(jnp.int32, (rows, cols), 0),
        lax.broadcasted_iota(jnp.int32, (rows, cols), 1),
    )


def band(index):
    one = jnp.int32(1)
    zero = jnp.int32(0)
    total = jnp.zeros_like(index)
    for k in range(1, GROUP):
        total = total + jnp.where(index >= k * B, one, zero)
    return total


def hot(condition):
    return jnp.where(condition, 1.0, 0.0).astype(BF16)


def twice(table):
    return jnp.concatenate([table, table], axis=1)


def kernel(
    slabs,
    corners,
    pairs,
    count,
    eigen,
    orb,
    ext,
    left,
    into,
    outof,
    wide_h,
    wide_l,
    narrow_h,
    narrow_l,
    near,
    column,
    level_bc,
    out,
    obx,
    nxt,
    moved,
    spec,
    pencil,
    turned,
    solved,
    win,
    mate,
    came,
    fw,
    ret,
    back,
    flag,
    told,
    dz_to,
    dz_from,
    dx_to,
    dx_from,
    put_z,
    get_z,
    put_x,
    get_x,
    load_sem,
    box_s,
    box_r,
    halo_s,
    halo_r,
    one_s,
    one_r,
    one_o,
    two_s,
    two_r,
    two_o,
    ret_s,
    ret_r,
    flag_s,
    flag_r,
    mate_s,
    mate_r,
    den_s,
    den_r,
    fld_s,
    fld_r,
    give_s,
    give_r,
):
    slab = lax.axis_index("slab")
    sub = lax.axis_index("sub")
    ahead = lax.rem(slab + 1, slabs)
    behind = lax.rem(slab + slabs - 1, slabs)
    ahead2 = lax.rem(slab + 2, slabs)
    behind2 = lax.rem(slab + slabs - 2, slabs)
    odd = lax.rem(slab, 2)
    partner = slab + 1 - 2 * odd
    planes = slabs * SX
    orbitals = 2 * slabs

    load = pltpu.make_async_copy(orb, obx.at[:, :, EDGE : EDGE + ROWS * B], load_sem)
    load.start()
    mate[0] = jnp.zeros((SX, ROWS * GZ), F32)
    mate[HOPS] = jnp.zeros((SX, ROWS * GZ), F32)
    win[REACH] = jnp.zeros((SX, ROWS * GZ), F32)
    barrier = pltpu.get_barrier_semaphore()
    for who in (ahead, behind, ahead2, behind2):
        pl.semaphore_signal(barrier, inc=1, device_id=(who, sub), device_id_type=MESH)
    for k in range(1, SUBS):
        pl.semaphore_signal(
            barrier, inc=1, device_id=(slab, lax.rem(sub + k, SUBS)), device_id_type=MESH
        )

    def remote(src, dst, send, recv, who):
        return pltpu.make_async_remote_copy(
            src_ref=src,
            dst_ref=dst,
            send_sem=send,
            recv_sem=recv,
            device_id=who,
            device_id_type=MESH,
        )

    def box_lanes(g):
        return pl.ds(pl.multiple_of(g * LANES, 128), LANES)

    def own_lanes(g):
        return pl.ds(pl.multiple_of(EDGE + g * LANES, 128), LANES)

    def grid_lanes(g):
        return pl.ds(pl.multiple_of(g * GLANES, 128), GLANES)

    def box_copy(g):
        return remote(
            orb.at[:, :, box_lanes(g)],
            nxt.at[:, :, box_lanes(g)],
            box_s,
            box_r.at[g],
            (behind, sub),
        )

    def halo_copy(side):
        start = EDGE if side == 0 else ROWS * B
        land = EDGE + ROWS * B if side == 0 else 0
        who = lax.rem(sub + (SUBS - 1 if side == 0 else 1), SUBS)
        return remote(
            obx.at[:, :, start : start + EDGE],
            obx.at[:, :, land : land + EDGE],
            halo_s.at[side],
            halo_r.at[side],
            (slab, who),
        )

    def spec_rows(g):
        return pl.ds(pl.multiple_of(g * SLICE, 8), SLICE)

    def pencil_rows(g):
        return pl.ds(pl.multiple_of((sub * CHUNKS + g) * SLICE, 8), SLICE)

    def one_copy(k, s, g):
        who = lax.rem(sub + k, SUBS)
        return remote(
            spec.at[s, who, spec_rows(g)],
            pencil.at[s, pencil_rows(g)],
            one_s.at[k - 1],
            one_r.at[k - 1, s, g],
            (slab, who),
        )

    def one_own(s, g):
        return pltpu.make_async_copy(
            spec.at[s, sub, spec_rows(g)], pencil.at[s, pencil_rows(g)], one_o.at[s, g]
        )

    def turned_rows(who, g):
        return pl.ds(pl.multiple_of((who * CHUNKS + g) * SLICE, 8), SLICE)

    def two_copy(k, s, g):
        who = lax.rem(sub + k, SUBS)
        return remote(
            turned.at[s, turned_rows(who, g)],
            solved.at[s, sub, spec_rows(g)],
            two_s.at[k - 1],
            two_r.at[k - 1, s, g],
            (slab, who),
        )

    def two_own(s, g):
        return pltpu.make_async_copy(
            turned.at[s, turned_rows(sub, g)], solved.at[s, sub, spec_rows(g)], two_o.at[s, g]
        )

    def ret_copy(s, g):
        return remote(
            ret.at[s, :, box_lanes(g)],
            back.at[s, :, box_lanes(g)],
            ret_s,
            ret_r.at[s, g],
            (ahead, sub),
        )

    def flag_copy():
        return remote(flag, told, flag_s, flag_r, (ahead, sub))

    def mate_copy(k):
        return remote(
            win.at[2 * k + 1],
            mate.at[k + odd],
            mate_s,
            mate_r.at[k],
            (partner, sub),
        )

    def ring(c):
        return pl.ds(c * RL, RL)

    def den_copy(j, c):
        return remote(
            win.at[2 * (HOPS + 1 - j), :, ring(c)],
            came.at[HOPS - j, :, ring(c)],
            den_s,
            den_r.at[j - 1, c],
            (ahead2, sub),
        )

    def fld_copy(j, c):
        return remote(
            fw.at[2 * j - 1, :, ring(c)],
            fw.at[2 * j + 1, :, ring(c)],
            fld_s,
            fld_r.at[j - 1, c],
            (behind2, sub),
        )

    def give_copy(j):
        return remote(
            fw.at[2 * j + 1],
            fw.at[2 * j + 2 * odd],
            give_s,
            give_r.at[j],
            (partner, sub),
        )

    start_x = []
    start_z = []
    for o in range(2):
        mine = slab * 2 + o
        start_x.append(lax.rem(corners[0, mine] - slab * SX + planes, planes))
        start_z.append(corners[1, mine])
    first, second, weight, shift_x, shift_z = [], [], [], [], []
    for s in range(2):
        i, j = pairs[s, 0], pairs[s, 1]
        first.append(lax.rem(i - 2 * slab + orbitals, orbitals))
        second.append(lax.rem(j - 2 * slab + orbitals, orbitals))
        half = planes // 2
        shift_x.append(lax.rem(corners[0, j] - corners[0, i] + half + planes, planes) - half)
        shift_z.append(corners[1, j] - corners[1, i])
        weight.append(jnp.where(count[0] > s, jnp.float32(1.0), jnp.float32(0.0)))

    pl.semaphore_wait(barrier, 4 + SUBS - 1)

    def send_boxes(g, _):
        box_copy(g).start()
        return 0

    lax.fori_loop(0, CHUNKS, send_boxes, 0)
    for s in range(2):
        for k in range(2):
            mark = jnp.where(second[s] == 2 + k, jnp.float32(1.0), jnp.float32(0.0))
            flag[s, k] = jnp.zeros((8, 128), F32) + mark
    flag_copy().start()

    row, col = iotas(LANES, GLANES)
    at = col - row - 32 * band(row)
    for o in range(2):
        put_z[o] = hot(at == start_z[o])
    row, col = iotas(REACH * SX, B)
    at = row - col
    for o in range(2):
        put_x[:, 2 * o * B : (2 * o + 2) * B] = twice(hot(at == start_x[o]))

    load.wait()
    halo_copy(0).start()
    halo_copy(1).start()

    def deposit(g, _):
        parts = []
        for o in range(2):
            box = obx[o, :, own_lanes(g)]
            parts.append(pick1(box * box, put_z[o]))
        total = dot(put_x[...], jnp.concatenate(parts, axis=0))
        win[0:REACH, :, grid_lanes(g)] = total.reshape(REACH, SX, GLANES)
        return 0

    lax.fori_loop(0, CHUNKS, deposit, 0, unroll=2)

    def send_mate(k, _):
        mate_copy(HOPS - 1 - k).start()
        return 0

    lax.fori_loop(0, HOPS, send_mate, 0)

    row, col = iotas(LANES, LANES)
    same = band(row) == band(col)
    at = col - row
    for s in range(2):
        dz_to[s] = hot(same & (at == shift_z[s]))
    row, col = iotas(B, B)
    at = row - col
    for s in range(2):
        dx_to[s] = twice(hot(at == shift_x[s]))

    mate_copy(HOPS - 1).wait_recv()
    for c in range(RING):
        win[REACH, :, ring(c)] += mate[HOPS, :, ring(c)]
        den_copy(1, c).start()

    def density_step(j):
        m = HOPS + 1 - j
        mate_copy(HOPS - j).wait_recv()
        for c in range(RING):
            den_copy(j - 1, c).wait_recv()
            win[2 * m, :, ring(c)] += mate[m, :, ring(c)] + came[m, :, ring(c)]
            den_copy(j, c).start()

    halo_copy(0).wait_recv()
    halo_copy(1).wait_recv()
    keep_low = jnp.where(sub > 0, jnp.float32(1.0), jnp.float32(0.0))
    keep_high = jnp.where(sub < SUBS - 1, jnp.float32(1.0), jnp.float32(0.0))
    obx[:, :, 0:EDGE] = obx[:, :, 0:EDGE] * keep_low
    high_edge = EDGE + ROWS * B
    obx[:, :, high_edge : high_edge + EDGE] = obx[:, :, high_edge : high_edge + EDGE] * keep_high

    def forward(g, _):
        density_step(2 + g)
        parts = [split(obx[o, :, pl.ds(pl.multiple_of(g * LANES, 128), LANES + 2 * EDGE)]) for o in range(2)]
        beside = dot(
            jnp.concatenate([p[0] for p in parts] + [p[1] for p in parts], axis=0), near[...]
        )
        for o in range(2):
            inner = [p[:, EDGE : EDGE + LANES] for p in parts[o]]
            lap = dot(column[...], jnp.concatenate(inner, axis=0))
            lap = lap + beside[o * B : (o + 1) * B] + beside[(2 + o) * B : (3 + o) * B]
            out[o, :, box_lanes(g)] = -0.5 * lap
        box_copy(g).wait_recv()
        boxes = [obx[0, :, own_lanes(g)], obx[1, :, own_lanes(g)]]
        later = [nxt[0, :, box_lanes(g)], nxt[1, :, box_lanes(g)]]
        rhos = []
        for s in range(2):
            other = jnp.where(
                second[s] < 2,
                jnp.where(second[s] == 0, boxes[0], boxes[1]),
                jnp.where(second[s] == 2, later[0], later[1]),
            )
            shifted = dot(dx_to[s], pick1(other, dz_to[s]))
            moved[s, :, box_lanes(g)] = shifted
            rhos.append(jnp.where(first[s] == 0, boxes[0], boxes[1]) * shifted)
        wides = right3(rhos, wide_h[...], wide_l[...])
        for s in range(2):
            both = left3(left[...], wides[s])
            for m in range(PACK):
                rows = pl.ds(pl.multiple_of((g * PACK + m) * ROWS, 8), ROWS)
                for q in range(SUBS):
                    spec[s, q, rows, :] = both[q * ROWS : (q + 1) * ROWS, m * 128 : (m + 1) * 128]
            for k in (2, 1, 3):
                one_copy(k, s, g).start()
            one_own(s, g).start()
        return 0

    lax.fori_loop(0, CHUNKS, forward, 0)
    density_step(HOPS)

    for c in range(RING):
        den_copy(HOPS, c).wait_recv()
        value = win[0, :, ring(c)] + mate[0, :, ring(c)] + came[0, :, ring(c)] + EPSILON
        root = jnp.exp(jnp.log(value) * (1.0 / 3.0))
        root = root - (root * root * root - value) / (3.0 * root * root)
        fw[1, :, ring(c)] = ext[:, ring(c)] - LOCAL_FACTOR * root
        fld_copy(1, c).start()
    give_copy(0).start()

    def field_last():
        for c in range(RING):
            fld_copy(HOPS, c).wait_recv()
        give_copy(HOPS).start()

    def field_step(j):
        for c in range(RING):
            fld_copy(j, c).wait_recv()
            fld_copy(j + 1, c).start()
        give_copy(j).start()

    row, col = iotas(LANES, LANES)
    same = band(row) == band(col)
    at = col - row
    for s in range(2):
        dz_from[s] = hot(same & (at == -shift_z[s]))
    row, col = iotas(B, B)
    at = row - col
    for s in range(2):
        dx_from[s] = twice(hot(at == -shift_x[s]))
    row, col = iotas(GLANES, LANES)
    at = row - col - 32 * band(col)
    for o in range(2):
        get_z[o] = hot(at == start_z[o])
    row, col = iotas(B, REACH * SX)
    at = col - row
    for o in range(2):
        get_x[o * B : (o + 1) * B, :] = twice(hot(at == start_x[o]))
    lane = lax.broadcasted_iota(jnp.int32, (ROWS, 128), 1)

    def along_y(s, t):
        a = 2 * t
        pieces, values = [], []
        for m in range(2):
            level = eigen[sub * ROWS + a + m]
            pieces.append((4.0 * math.pi) / (level_bc[...] + level))
            tiles = [
                pencil[s, pl.ds(k * ROWS + a + m, SUBS * CHUNKS, stride=SLICE), :]
                for k in range(PACK)
            ]
            last = [pltpu.roll(tiles[k], 32 * (k + 1), 1) for k in range(PACK)]
            rest = jnp.where(lane < 32, last[0], jnp.where(lane < 64, last[1], last[2]))
            values.append(jnp.concatenate(tiles + [rest], axis=0))
        factor = jnp.concatenate(pieces, axis=1)
        value = left3(into[...], jnp.concatenate(values, axis=1))
        value = left3(outof[...], factor * value)
        for m in range(2):
            tile = value[:, m * 128 : (m + 1) * 128]
            rest = tile[PACK * ROWS :]
            for k in range(PACK):
                packed = jnp.where(
                    lane < B, tile[k * ROWS : (k + 1) * ROWS], pltpu.roll(rest, B - 32 * k, 1)
                )
                turned[s, pl.ds(k * ROWS + a + m, SUBS * CHUNKS, stride=SLICE), :] = packed

    def middle(s):
        def wait_one(g, _):
            for k in range(1, SUBS):
                one_copy(k, s, g).wait_recv()
            one_own(s, g).wait()
            return 0

        def turn(t, _):
            along_y(s, t)
            return 0

        def send_two(g, _):
            for k in (2, 1, 3):
                two_copy(k, s, g).start()
            two_own(s, g).start()
            return 0

        lax.fori_loop(0, CHUNKS, wait_one, 0)
        lax.fori_loop(0, ROWS // 2, turn, 0, unroll=2)
        lax.fori_loop(0, CHUNKS, send_two, 0)

    middle(0)
    field_step(1)
    middle(1)

    def inverse(s, g):
        for k in range(1, SUBS):
            two_copy(k, s, g).wait_recv()
        two_own(s, g).wait()
        pieces = []
        for m in range(PACK):
            rows = pl.ds(pl.multiple_of((g * PACK + m) * ROWS, 8), ROWS)
            pieces.append(jnp.concatenate([solved[s, q, rows, :] for q in range(SUBS)], axis=0))
        spread = left3(left[...], jnp.concatenate(pieces, axis=1))
        potential = right3([spread], narrow_h[...], narrow_l[...])[0]
        potential = potential * (weight[s] * FOCK_SHARE)
        onto_first = potential * moved[s, :, box_lanes(g)]
        box = jnp.where(first[s] == 0, obx[0, :, own_lanes(g)], obx[1, :, own_lanes(g)])
        onto_second = dot(dx_from[s], pick1(potential * box, dz_from[s]))
        ret[s, :, box_lanes(g)] = onto_second
        ret_copy(s, g).start()
        for k in range(2):
            out[k, :, box_lanes(g)] -= jnp.where(first[s] == k, onto_first, 0.0) + jnp.where(
                second[s] == k, onto_second, 0.0
            )

    field_step(2)

    def two_chunks(s, first_step):
        def body(p, _):
            field_step(first_step + p)
            inverse(s, 2 * p)
            inverse(s, 2 * p + 1)
            return 0

        return body

    lax.fori_loop(0, CHUNKS // 2, two_chunks(0, 3), 0)
    lax.fori_loop(0, CHUNKS // 2 - 1, two_chunks(1, 3 + CHUNKS // 2), 0)
    field_last()
    inverse(1, CHUNKS - 2)
    inverse(1, CHUNKS - 1)
    flag_copy().wait_recv()

    def wait_give(j, _):
        give_copy(j).wait_recv()
        return 0

    lax.fori_loop(0, HOPS + 1, wait_give, 0)

    def finish(g, _):
        field = fw[1 : REACH + 1, :, grid_lanes(g)].reshape(REACH * SX, GLANES)
        local = dot(get_x[...], stack(field))
        for s in range(2):
            ret_copy(s, g).wait_recv()
        came_back = [back[s, :, box_lanes(g)] for s in range(2)]
        for o in range(2):
            here = right1(local[o * B : (o + 1) * B], get_z[o])
            total = here * obx[o, :, own_lanes(g)]
            for s in range(2):
                marks = jnp.concatenate([told[s, o]] * (LANES // 128), axis=1)
                marks = jnp.concatenate([marks] * (B // 8), axis=0)
                total = total - marks * came_back[s]
            out[o, :, box_lanes(g)] += total
        return 0

    lax.fori_loop(0, CHUNKS, finish, 0, unroll=2)

    remote(orb, nxt, box_s, box_r.at[0], (behind, sub)).wait_send()
    remote(ret, back, ret_s, ret_r.at[0, 0], (ahead, sub)).wait_send()
    flag_copy().wait_send()
    for k in range(1, SUBS):
        who = lax.rem(sub + k, SUBS)
        whole = solved.at[:, 0]
        remote(whole, whole, one_s.at[k - 1], one_r.at[0, 0, 0], (slab, who)).wait_send()
        remote(whole, whole, two_s.at[k - 1], two_r.at[0, 0, 0], (slab, who)).wait_send()
    halo_copy(0).wait_send()
    halo_copy(1).wait_send()
    eight = win.at[0:HOPS]
    nine = win.at[0 : HOPS + 1]
    remote(eight, came, mate_s, mate_r.at[0], (partner, sub)).wait_send()
    remote(eight, came, den_s, den_r.at[0, 0], (ahead2, sub)).wait_send()
    remote(eight, came, fld_s, fld_r.at[0, 0], (behind2, sub)).wait_send()
    remote(nine, mate, give_s, give_r.at[0], (partner, sub)).wait_send()


def local(slabs, orbitals, external_potential, corners, pair_list, pair_count):
    vmem = pl.BlockSpec(memory_space=pltpu.VMEM)
    smem = pl.BlockSpec(memory_space=pltpu.SMEM)
    table = tables()
    arrays = [jnp.asarray(t) for t in table[:-1]]
    eigen = jnp.asarray(table[-1])
    dma = pltpu.SemaphoreType.DMA
    part = (2, B, ROWS * B)
    parted = (2, SUBS, CHUNKS * SLICE, 128)
    joined = (2, SUBS * CHUNKS * SLICE, 128)
    block = (SX, ROWS * GZ)
    return pl.pallas_call(
        functools.partial(kernel, slabs),
        out_shape=jax.ShapeDtypeStruct(orbitals.shape, F32),
        in_specs=[smem] * 4 + [pl.BlockSpec(memory_space=pl.ANY)] + [vmem] * (1 + len(arrays)),
        out_specs=vmem,
        scratch_shapes=[
            pltpu.VMEM((2, B, ROWS * B + 2 * EDGE), F32),
            pltpu.VMEM(part, F32),
            pltpu.VMEM(part, F32),
            pltpu.VMEM(parted, F32),
            pltpu.VMEM(joined, F32),
            pltpu.VMEM(joined, F32),
            pltpu.VMEM(parted, F32),
            pltpu.VMEM((REACH + 1,) + block, F32),
            pltpu.VMEM((HOPS + 1,) + block, F32),
            pltpu.VMEM((HOPS,) + block, F32),
            pltpu.VMEM((REACH + 3,) + block, F32),
            pltpu.VMEM(part, F32),
            pltpu.VMEM(part, F32),
            pltpu.VMEM((2, 2, 8, 128), F32),
            pltpu.VMEM((2, 2, 8, 128), F32),
            pltpu.VMEM((2, LANES, LANES), BF16),
            pltpu.VMEM((2, LANES, LANES), BF16),
            pltpu.VMEM((2, B, 2 * B), BF16),
            pltpu.VMEM((2, B, 2 * B), BF16),
            pltpu.VMEM((2, LANES, GLANES), BF16),
            pltpu.VMEM((2, GLANES, LANES), BF16),
            pltpu.VMEM((REACH * SX, 4 * B), BF16),
            pltpu.VMEM((2 * B, 2 * REACH * SX), BF16),
            dma,
            dma,
            dma((CHUNKS,)),
            dma((2,)),
            dma((2,)),
            dma((SUBS - 1,)),
            dma((SUBS - 1, 2, CHUNKS)),
            dma((2, CHUNKS)),
            dma((SUBS - 1,)),
            dma((SUBS - 1, 2, CHUNKS)),
            dma((2, CHUNKS)),
            dma,
            dma((2, CHUNKS)),
            dma,
            dma,
            dma,
            dma((HOPS,)),
            dma,
            dma((HOPS, RING)),
            dma,
            dma((HOPS, RING)),
            dma,
            dma((HOPS + 1,)),
        ],
        compiler_params=pltpu.CompilerParams(
            collective_id=0, has_side_effects=True, vmem_limit_bytes=60 * 1024 * 1024
        ),
        name="orbitals",
    )(corners.T, pair_list, pair_count, eigen, orbitals, external_potential, *arrays)


def solution(mesh):
    placed = (P("slab", None, "sub"), P("slab", "sub"), P(), P("slab", None), P("slab"))
    return jax.shard_map(
        functools.partial(local, mesh.shape["slab"]),
        mesh=mesh,
        in_specs=placed,
        out_specs=P("slab", None, "sub"),
        check_vma=False,
    )
```
